1024 devices in a mesh: dp: 64 (over y, x, core), section: 16 (over z).
Axes of the slice: x: 4, y: 8, z: 16, core: 2. Of those that a mesh axis runs over, the one named last changes fastest.
Arguments:
- inputs: bfloat16 [8192, 3072], P('dp'), may hold values from -6 to 6
- tiles: bfloat16 [16, 72, 128, 128], P('section'), may hold values from -0.3125 to 0.3125
- tile_rows: int32 [16, 72], P('section'), may hold values from 0 to 23, as said below
- out_grad: bfloat16 [8192, 3072], P('dp'), may hold values from -0.119628906 to 0.119628906
Outputs:
- weight_grad: float32 [128, 16, 72, 128], P('dp', 'section')
The draws below stay inside these ranges and needn't reach their ends.
Inputs may be any that keep to these rules, and one draw needn't show every extreme that they name: `tile_rows`: in each layer, the 3 entries of every aligned group of 3 consecutive tiles (one tile column) name different tile rows.
All inputs are finite; a program needn't handle non-finite values.
Results may differ from the reference program's by a relative error of at most 0.025.
Values may be sent and summed in bfloat16 or wider, within the bound.
A program may use at most 32 MiB of HBM per device.

```python
import jax
import jax.numpy as jnp
from jax import lax

E = 3072
BLOCK = 128
MB = 32
NMB = 4
NB = 24
KPC = 3
NT = 72
LAYERS = 16
ROWS = 8192


def draw_tile_rows(key, part):
    keys = jax.random.split(key, LAYERS * NB)

    def pick_rows(single):
        return jax.random.permutation(single, NB)[:KPC]
    chosen = jax.vmap(pick_rows)(keys)
    return chosen.reshape(LAYERS, NB * KPC).astype(jnp.int32)


def level_of(rng, shape, cuts, smallest, high):
    def one(axis_at, blocks):
        heights = jax.random.uniform(jax.random.fold_in(jax.random.fold_in(rng, 6), axis_at), (blocks,), jnp.float32, smallest / len(cuts), high / len(cuts))
        return jnp.repeat(jnp.exp(heights), shape[axis_at] // blocks).reshape((-1,) + (1,) * (len(shape) - axis_at - 1))

    gain = one(*cuts[0])
    for cut in cuts[1:]:
        gain = gain * one(*cut)
    return gain


def gaussian(stream_key, extent, scale, limit, cuts=(), kind=jnp.bfloat16):
    values = jax.random.normal(stream_key, extent, jnp.float32) * scale
    if len(cuts) > 0:
        values = level_of(stream_key, extent, cuts, -0.22, 0.18) * values
    return jnp.clip(values, min=-limit, max=limit).astype(kind)


def setup_inputs(seed: int = 0) -> dict:
    splits = jax.random.split(jax.random.key(seed), 5)
    return {
        "inputs": gaussian(splits[0], (ROWS, E), 1.0, 6.0, ((0, 64),)),
        "tiles": gaussian(splits[1], (LAYERS, NT, BLOCK, BLOCK), (KPC * BLOCK) ** -0.5, 0.3125, ((0, 16),)),
        "tile_rows": draw_tile_rows(jax.random.fold_in(splits[4], 71), 0),
        "out_grad": gaussian(splits[3], (ROWS, E), 0.02, 0.119628906, ((0, 64),)),
    }


EPS = 1e-06

def layer_forward(h, tile_set, rows, nb, kpc):
    count = h.shape[0]
    blk = tile_set.shape[-1]
    hf = h.astype(jnp.float32)
    scale = lax.rsqrt(lax.optimization_barrier(jnp.mean(hf * hf, axis=1, keepdims=True)) + EPS)
    low = (hf * scale).astype(jnp.bfloat16)
    picked = jnp.take(low.reshape(count, nb, blk), rows, axis=1).astype(jnp.float32)
    parts = jnp.einsum('mtr,trc->mtc', picked, tile_set.astype(jnp.float32), precision=lax.Precision.HIGHEST)
    mixed = parts.reshape(count, nb, kpc, blk).sum(axis=2).reshape(count, nb * blk)
    act = jnp.tanh(mixed)
    out = (hf + act).astype(jnp.bfloat16)
    return (out, scale, act)

def layer_backward(h, scale, act, grad, tile_set, rows, nb, kpc):
    count = h.shape[0]
    blk = tile_set.shape[-1]
    gradf = grad.astype(jnp.float32)
    dz = (gradf * (1.0 - act * act)).astype(jnp.bfloat16)
    back = jnp.einsum('mnc,nkrc->mnkr', dz.reshape(count, nb, blk).astype(jnp.float32), tile_set.reshape(nb, kpc, blk, blk).astype(jnp.float32), precision=lax.Precision.HIGHEST)
    onehot = (rows[:, None] == jnp.arange(nb, dtype=jnp.int32)[None, :]).astype(jnp.float32)
    spread = jnp.einsum('mtr,tb->mbr', back.reshape(count, nb * kpc, blk), onehot, precision=lax.Precision.HIGHEST).reshape(count, nb * blk)
    normed = h.astype(jnp.float32) * scale
    inner = lax.optimization_barrier(jnp.mean(spread * normed, axis=1, keepdims=True))
    result = gradf + scale * (spread - normed * inner)
    return (dz, result.astype(jnp.bfloat16))

def weight_term(h, scale, dz, rows, nb, kpc, blk):
    count = h.shape[0]
    low = (h.astype(jnp.float32) * scale).astype(jnp.bfloat16)
    picked = jnp.take(low.reshape(count, nb, blk), rows, axis=1).reshape(count, nb, kpc, blk)
    term = jnp.einsum('mnkr,mnc->rnkc', picked.astype(jnp.float32), dz.reshape(count, nb, blk).astype(jnp.float32), precision=lax.Precision.HIGHEST)
    return term.reshape(blk, nb * kpc, blk)

def reference(inputs, tiles, tile_rows, out_grad):
    width = inputs.shape[1]
    groups = inputs.shape[0] // (NMB * MB)
    feed = inputs.reshape(groups, NMB * MB, width)
    seeds = out_grad.reshape(groups, NMB * MB, width)

    def one_group(total, pair):
        h, grad = pair
        saved = []
        for layer in range(LAYERS):
            out, scale, act = layer_forward(h, tiles[layer], tile_rows[layer], NB, KPC)
            saved.append((h, scale, act))
            h = out
        for layer in reversed(range(LAYERS)):
            h_in, scale, act = saved[layer]
            dz, grad = layer_backward(h_in, scale, act, grad, tiles[layer], tile_rows[layer], NB, KPC)
            term = weight_term(h_in, scale, dz, tile_rows[layer], NB, KPC, BLOCK)
            total = total.at[:, layer].add(term)
        return (total, None)
    start = jnp.zeros((BLOCK, LAYERS, NT, BLOCK), jnp.float32)
    total, unused = lax.scan(one_group, start, (feed, seeds))
    return total
```

```python
import functools

import jax
import jax.numpy as jnp
from jax import lax
from jax.experimental import pallas as pl
from jax.experimental.pallas import tpu as pltpu
from jax.sharding import PartitionSpec as P

EPS = 1e-06
MB = 8
CHUNKS = 2
GRID_X = 4
GRID_Y = 8
GROUPS = 3
MESH = pl.DeviceIdType.MESH
F32 = jnp.float32
BF16 = jnp.bfloat16


def relay_kernel(sections, nmb, nb, rows_ref, perm_ref, last_ref, keep_ref, full_ref, x_ref, t_ref, og_ref,
                 u_ref, dz_ref,
                 hbuf, gbuf, fout, gout, hw, act, scl, prod, pref,
                 fsend, frecv, bsend, brecv):
    sec = lax.axis_index("section")
    width = nb * 128
    per = nb // CHUNKS
    first = sec == 0
    final = sec == sections - 1
    up = jnp.minimum(sec + 1, sections - 1)
    down = jnp.maximum(sec - 1, 0)

    barrier = pltpu.get_barrier_semaphore()

    @pl.when(sec > 0)
    def _():
        pl.semaphore_signal(barrier, inc=1, device_id={"section": down}, device_id_type=MESH)

    @pl.when(sec < sections - 1)
    def _():
        pl.semaphore_signal(barrier, inc=1, device_id={"section": up}, device_id_type=MESH)

    near = jnp.where(first, 0, 1) + jnp.where(final, 0, 1)
    pl.semaphore_wait(barrier, near)

    def fcopy(k, j):
        return pltpu.make_async_remote_copy(
            src_ref=fout.at[k, pl.ds(j * per, per)],
            dst_ref=hbuf.at[k, pl.ds(j * per, per)],
            send_sem=fsend.at[k],
            recv_sem=frecv.at[k],
            device_id={"section": up},
            device_id_type=MESH,
        )

    def bcopy(k, j):
        return pltpu.make_async_remote_copy(
            src_ref=gout.at[k, pl.ds(j * per, per)],
            dst_ref=gbuf.at[k, pl.ds(j * per, per)],
            send_sem=bsend.at[k],
            recv_sem=brecv.at[k],
            device_id={"section": down},
            device_id_type=MESH,
        )

    def fwhole(k):
        return pltpu.make_async_remote_copy(
            src_ref=fout.at[k], dst_ref=hbuf.at[k], send_sem=fsend.at[k], recv_sem=frecv.at[k],
            device_id={"section": up}, device_id_type=MESH,
        )

    def bwhole(k):
        return pltpu.make_async_remote_copy(
            src_ref=gout.at[k], dst_ref=gbuf.at[k], send_sem=bsend.at[k], recv_sem=brecv.at[k],
            device_id={"section": down}, device_id_type=MESH,
        )

    def forward(k, carry):
        @pl.when(first)
        def _():
            hbuf[k] = x_ref[k]

        @pl.when(sec > 0)
        def _():
            fwhole(k).wait_recv()

        total = jnp.zeros((MB, 128), F32)
        for b in range(nb):
            h = hbuf[k, b]
            hf = h.astype(F32)
            total = total + hf * hf
            hw[b] = h
        mean = jnp.sum(total, axis=1, keepdims=True) * (1.0 / width)
        scale = jnp.broadcast_to(lax.rsqrt(mean + EPS), (MB, 128))
        scl[k] = scale
        for c in range(nb):
            left = jnp.concatenate([hw[rows_ref[3 * c + i]] for i in range(3)], axis=1)
            z = jnp.dot(left, t_ref[c], preferred_element_type=F32)
            a = jnp.tanh(z * scale)
            act[k, c] = 1.0 - a * a
            fout[k, c] = (hbuf[k, c].astype(F32) + a).astype(BF16)
            if (c + 1) % per == 0:
                @pl.when(sec < sections - 1)
                def _(j=c // per):
                    fcopy(k, j).start()
        return carry

    lax.fori_loop(0, nmb, forward, 0)

    def backward(k, carry):
        @pl.when(final)
        def _():
            gbuf[k] = og_ref[k]

        @pl.when(sec < sections - 1)
        def _():
            bwhole(k).wait_recv()

        for c in range(nb):
            dz = (gbuf[k, c].astype(F32) * act[k, c]).astype(BF16)
            dz_ref[k, c] = dz
            back = lax.dot_general(dz, t_ref[c], (((1,), (1,)), ((), ())), preferred_element_type=F32)
            for i in range(3):
                prod[3 * c + i] = back[:, i * 128:(i + 1) * 128]
        scale = scl[k]
        acc = jnp.zeros((MB, 128), F32)
        for i in range(3 * nb):
            acc = acc * keep_ref[i] + prod[perm_ref[i]]
            pref[i] = acc
        inner = jnp.zeros((MB, 128), F32)
        for b in range(nb):
            q = hbuf[k, b].astype(F32) * scale
            u_ref[k, b] = q.astype(BF16)
            v = pref[last_ref[b]] * full_ref[b]
            inner = inner + v * q
            hw2 = v
            prod[b] = hw2
        inner = jnp.sum(inner, axis=1, keepdims=True) * (1.0 / width)
        inner = jnp.broadcast_to(inner, (MB, 128))
        for b in range(nb):
            q = hbuf[k, b].astype(F32) * scale
            g = gbuf[k, b].astype(F32) + scale * (prod[b] - q * inner)
            gout[k, b] = g.astype(BF16)
            if (b + 1) % per == 0:
                @pl.when(sec > 0)
                def _(j=b // per):
                    bcopy(k, j).start()
        return carry

    lax.fori_loop(0, nmb, backward, 0)

    def drain(k, carry):
        @pl.when(sec < sections - 1)
        def _():
            fwhole(k).wait_send()

        @pl.when(sec > 0)
        def _():
            bwhole(k).wait_send()

        return carry

    lax.fori_loop(0, nmb, drain, 0)


def reduce_kernel(gx, gy, nb, nmb, rows_ref, u_ref, dz_ref, out_ref,
                  ut, dzl, own, other, got0, sx, got1, sy, got2,
                  s0, r0, s1, r1, s2, r2):
    nt = 3 * nb
    ni = 128 // (2 * gx * gy)
    rx = gy * ni
    per = nt // GROUPS
    sub = per // 8
    dp = lax.axis_index("dp")
    me_c = lax.rem(dp, 2)
    me_x = lax.rem(dp // 2, gx)
    me_y = dp // (2 * gx)

    def at(y, x, c):
        return {"dp": (y * gx + x) * 2 + c}

    mate = at(me_y, me_x, 1 - me_c)
    xs = [at(me_y, lax.rem(me_x + j, gx), me_c) for j in range(1, gx)]
    ys = [at(lax.rem(me_y + j, gy), me_x, me_c) for j in range(1, gy)]

    barrier = pltpu.get_barrier_semaphore()
    for peer in [mate] + xs + ys:
        pl.semaphore_signal(barrier, inc=1, device_id=peer, device_id_type=MESH)

    p = lax.broadcasted_iota(jnp.int32, (128, 128), 0)
    r = lax.broadcasted_iota(jnp.int32, (128, 128), 1)
    far = p // 64
    core = far + me_c - 2 * far * me_c
    px = lax.rem(p // rx, gx)
    py = lax.rem(p // ni, gy)
    want = ((py * gx + px) * 2 + core) * ni + lax.rem(p, ni)
    order = jnp.where(r == want, 1.0, 0.0).astype(BF16)

    def prepare(b, carry):
        u = u_ref[:, b].astype(F32).reshape(nmb * MB, 128).astype(BF16)
        turned = lax.dot_general(order, u, (((1,), (1,)), ((), ())), preferred_element_type=F32)
        ut[b] = turned.astype(BF16)
        dzl[b] = dz_ref[:, b].astype(F32).reshape(nmb * MB, 128).astype(BF16)
        return carry

    lax.fori_loop(0, nb, prepare, 0)
    pl.semaphore_wait(barrier, gx + gy - 1)

    def copy0(g):
        return pltpu.make_async_remote_copy(
            src_ref=other.at[g], dst_ref=got0.at[g], send_sem=s0.at[g], recv_sem=r0.at[g],
            device_id=mate, device_id_type=MESH,
        )

    def copy1(g, j):
        return pltpu.make_async_remote_copy(
            src_ref=sx.at[g, j - 1], dst_ref=got1.at[g, j - 1], send_sem=s1.at[g, j - 1], recv_sem=r1.at[g, j - 1],
            device_id=xs[j - 1], device_id_type=MESH,
        )

    def copy2(g, j):
        return pltpu.make_async_remote_copy(
            src_ref=sy.at[g, lax.rem(me_y + j, gy)], dst_ref=got2.at[g, j - 1],
            send_sem=s2.at[g, j - 1], recv_sem=r2.at[g, j - 1],
            device_id=ys[j - 1], device_id_type=MESH,
        )

    for g in range(GROUPS):
        def column(c, carry, g=g):
            col = g * (per // 3) + c
            d = dzl[col]
            for i in range(3):
                full = jnp.dot(ut[rows_ref[3 * col + i]], d, preferred_element_type=F32)
                for x in range(gx):
                    own[g, x, 3 * c + i] = full[x * rx:(x + 1) * rx]
                    other[g, x, 3 * c + i] = full[64 + x * rx:64 + (x + 1) * rx].astype(BF16)
            return carry

        lax.fori_loop(0, per // 3, column, 0)
        copy0(g).start()

    for g in range(GROUPS):
        copy0(g).wait_recv()
        for j in range(1, gx):
            dest = lax.rem(me_x + j, gx)

            def fold(t, carry, g=g, j=j, dest=dest):
                sx[g, j - 1, t] = (own[g, dest, t] + got0[g, dest, t].astype(F32)).astype(BF16)
                return carry

            lax.fori_loop(0, per, fold, 0, unroll=4)
            copy1(g, j).start()

    a = lax.broadcasted_iota(jnp.int32, (8 * rx, 8 * rx), 0)
    b = lax.broadcasted_iota(jnp.int32, (8 * rx, 8 * rx), 1)
    src = lax.rem(a, 8) * rx + (a // (8 * ni)) * ni + lax.rem(a // 8, ni)
    mix = jnp.where(b == src, 1.0, 0.0).astype(BF16)

    for g in range(GROUPS):
        for j in range(1, gx):
            copy1(g, j).wait_recv()

        def block(q, carry, g=g):
            pieces = []
            for t in range(8):
                s = own[g, me_x, q * 8 + t] + got0[g, me_x, q * 8 + t].astype(F32)
                for j in range(gx - 1):
                    s = s + got1[g, j, q * 8 + t].astype(F32)
                pieces.append(s)
            s = jnp.concatenate(pieces, axis=0).astype(BF16)
            moved = jnp.dot(mix, s, preferred_element_type=F32).astype(BF16)
            for y in range(gy):
                sy[g, y, q] = moved[y * 8 * ni:(y + 1) * 8 * ni]
            return carry

        lax.fori_loop(0, sub, block, 0)
        for j in range(1, gy):
            copy2(g, j).start()

    for g in range(GROUPS):
        for j in range(1, gy):
            copy2(g, j).wait_recv()
        for q in range(sub):
            s = sy[g, me_y, q].astype(F32)
            for j in range(gy - 1):
                s = s + got2[g, j, q].astype(F32)
            for i in range(ni):
                out_ref[i, (g * sub + q) * 8:(g * sub + q + 1) * 8, :] = s[i * 8:(i + 1) * 8]

    for g in range(GROUPS):
        copy0(g).wait_send()
        for j in range(1, gx):
            copy1(g, j).wait_send()
        for j in range(1, gy):
            copy2(g, j).wait_send()


def tables(rows, nb):
    nt = rows.shape[0]
    spot = jnp.arange(nt, dtype=jnp.int32)
    before = (rows[None, :] < rows[:, None]) | ((rows[None, :] == rows[:, None]) & (spot[None, :] < spot[:, None]))
    rank = jnp.sum(before.astype(jnp.int32), axis=1)
    perm = jnp.sum(jnp.where(rank[None, :] == spot[:, None], spot[None, :], 0), axis=1)
    ordered = jnp.sum(jnp.where(rank[None, :] == spot[:, None], rows[None, :], 0), axis=1)
    previous = jnp.sum(jnp.where(rank[None, :] == spot[:, None] - 1, rows[None, :] + 1, 0), axis=1) - 1
    keep = jnp.where(ordered == previous, 1.0, 0.0).astype(F32)
    place = jnp.arange(nb, dtype=jnp.int32)
    upto = jnp.sum((rows[None, :] <= place[:, None]).astype(jnp.int32), axis=1)
    count = jnp.sum((rows[None, :] == place[:, None]).astype(jnp.int32), axis=1)
    return perm, jnp.maximum(upto - 1, 0), keep, (count > 0).astype(F32)


def local(gx, gy, inputs, tiles, tile_rows, out_grad):
    sections = lax.axis_size("section")
    rows = tile_rows[0]
    total, width = inputs.shape
    nb = width // 128
    nt = tiles.shape[1]
    nmb = total // MB
    feed = inputs.reshape(nmb, MB, nb, 128).transpose(0, 2, 1, 3)
    seeds = out_grad.reshape(nmb, MB, nb, 128).transpose(0, 2, 1, 3)
    tall = tiles.reshape(nb, 3 * 128, 128)
    perm, last, keep, full = tables(rows, nb)
    smem = pl.BlockSpec(memory_space=pltpu.SMEM)
    vmem = pl.BlockSpec(memory_space=pltpu.VMEM)
    dma = pltpu.SemaphoreType.DMA
    piece = (nmb, nb, MB, 128)
    u, dz = pl.pallas_call(
        functools.partial(relay_kernel, sections, nmb, nb),
        out_shape=[jax.ShapeDtypeStruct(piece, BF16), jax.ShapeDtypeStruct(piece, BF16)],
        in_specs=[smem] * 5 + [vmem] * 3,
        out_specs=[vmem] * 2,
        scratch_shapes=[
            pltpu.VMEM(piece, BF16), pltpu.VMEM(piece, BF16), pltpu.VMEM(piece, BF16), pltpu.VMEM(piece, BF16),
            pltpu.VMEM((nb, MB, 128), BF16),
            pltpu.VMEM(piece, F32),
            pltpu.VMEM((nmb, MB, 128), F32),
            pltpu.VMEM((nt, MB, 128), F32),
            pltpu.VMEM((nt, MB, 128), F32),
            dma((nmb,)), dma((nmb,)), dma((nmb,)), dma((nmb,)),
        ],
        compiler_params=pltpu.CompilerParams(collective_id=0, has_side_effects=True),
        name="relay",
    )(rows, perm, last, keep, full, feed, tall, seeds)
    ni = 128 // (2 * gx * gy)
    rx = gy * ni
    per = nt // GROUPS
    return pl.pallas_call(
        functools.partial(reduce_kernel, gx, gy, nb, nmb),
        out_shape=jax.ShapeDtypeStruct((ni, nt, 128), F32),
        in_specs=[smem] + [vmem] * 2,
        out_specs=vmem,
        scratch_shapes=[
            pltpu.VMEM((nb, 128, nmb * MB), BF16),
            pltpu.VMEM((nb, nmb * MB, 128), BF16),
            pltpu.VMEM((GROUPS, gx, per, rx, 128), F32),
            pltpu.VMEM((GROUPS, gx, per, rx, 128), BF16),
            pltpu.VMEM((GROUPS, gx, per, rx, 128), BF16),
            pltpu.VMEM((GROUPS, gx - 1, per, rx, 128), BF16),
            pltpu.VMEM((GROUPS, gx - 1, per, rx, 128), BF16),
            pltpu.VMEM((GROUPS, gy, per // 8, 8 * ni, 128), BF16),
            pltpu.VMEM((GROUPS, gy - 1, per // 8, 8 * ni, 128), BF16),
            dma((GROUPS,)), dma((GROUPS,)),
            dma((GROUPS, gx - 1)), dma((GROUPS, gx - 1)),
            dma((GROUPS, gy - 1)), dma((GROUPS, gy - 1)),
        ],
        compiler_params=pltpu.CompilerParams(collective_id=1, has_side_effects=True),
        name="reduce",
    )(rows, u, dz).reshape(ni, 1, nt, 128)


def solution(mesh, gx=GRID_X, gy=GRID_Y):
    return jax.shard_map(
        functools.partial(local, gx, gy),
        mesh=mesh,
        in_specs=(P("dp", None), P("section", None, None, None), P("section", None), P("dp", None)),
        out_specs=P("dp", "section", None, None),
        check_vma=False,
    )
```

```python
import functools

import jax
import jax.numpy as jnp
from jax import lax
from jax.experimental import pallas as pl
from jax.experimental.pallas import tpu as pltpu
from jax.sharding import PartitionSpec as P

EPS = 1e-06
MB = 8
CHUNKS = 2
CHAINS = 2
AHEAD = 6
GRID_X = 4
GRID_Y = 8
GROUPS = 3
MESH = pl.DeviceIdType.MESH
F32 = jnp.float32
BF16 = jnp.bfloat16


def arrange(gx, gy):
    ni = 128 // (2 * gx * gy)
    rx = gy * ni
    side = lax.rem(lax.axis_index("dp"), 2)
    p = lax.broadcasted_iota(jnp.int32, (128, 128), 0)
    r = lax.broadcasted_iota(jnp.int32, (128, 128), 1)
    far = p // 64
    core = far + side - 2 * far * side
    px = lax.rem(p // rx, gx)
    py = lax.rem(p // ni, gy)
    want = ((py * gx + px) * 2 + core) * ni + lax.rem(p, ni)
    return jnp.where(r == want, 1.0, 0.0).astype(BF16)


def relay_kernel(sections, nmb, nb, gx, gy, rows_ref, line_ref, x_ref, t_ref, og_ref,
                 ut_ref, dz_ref,
                 hbuf, gbuf, fout, gout, hw, act, scl, prod, pref, flip, board, table, tsem,
                 fsend, frecv, bsend, brecv):
    sec = lax.axis_index("section")
    nt = 3 * nb
    width = nb * 128
    per = nb // CHUNKS
    run = nt // CHAINS
    first = sec == 0
    final = sec == sections - 1
    up = jnp.minimum(sec + 1, sections - 1)
    down = jnp.maximum(sec - 1, 0)

    barrier = pltpu.get_barrier_semaphore()

    @pl.when(sec > 0)
    def _():
        pl.semaphore_signal(barrier, inc=1, device_id={"section": down}, device_id_type=MESH)

    @pl.when(sec < sections - 1)
    def _():
        pl.semaphore_signal(barrier, inc=1, device_id={"section": up}, device_id_type=MESH)

    near = jnp.where(first, 0, 1) + jnp.where(final, 0, 1)
    pl.semaphore_wait(barrier, near)

    def fcopy(k, j):
        return pltpu.make_async_remote_copy(
            src_ref=fout.at[k, pl.ds(j * per, per)],
            dst_ref=hbuf.at[k, pl.ds(j * per, per)],
            send_sem=fsend.at[k],
            recv_sem=frecv.at[k],
            device_id={"section": up},
            device_id_type=MESH,
        )

    def bcopy(k, j):
        return pltpu.make_async_remote_copy(
            src_ref=gout.at[k, pl.ds(j * per, per)],
            dst_ref=gbuf.at[k, pl.ds(j * per, per)],
            send_sem=bsend.at[k],
            recv_sem=brecv.at[k],
            device_id={"section": down},
            device_id_type=MESH,
        )

    def fwhole(k):
        return pltpu.make_async_remote_copy(
            src_ref=fout.at[k], dst_ref=hbuf.at[k], send_sem=fsend.at[k], recv_sem=frecv.at[k],
            device_id={"section": up}, device_id_type=MESH,
        )

    def bwhole(k):
        return pltpu.make_async_remote_copy(
            src_ref=gout.at[k], dst_ref=gbuf.at[k], send_sem=bsend.at[k], recv_sem=brecv.at[k],
            device_id={"section": down}, device_id_type=MESH,
        )

    def setup():
        ia = lax.broadcasted_iota(jnp.int32, (nt, nt), 0)
        ib = lax.broadcasted_iota(jnp.int32, (nt, nt), 1)
        across = jnp.broadcast_to(line_ref[...], (nt, nt))
        down_col = jnp.sum(jnp.where(ia == ib, across, 0), axis=1, keepdims=True)
        along = jnp.broadcast_to(down_col, (nt, nt))
        ahead = (across < along) | ((across == along) & (ib < ia))
        rank = jnp.broadcast_to(jnp.sum(jnp.where(ahead, 1, 0), axis=1, keepdims=True), (nt, nt))
        here = rank == ib
        perm = jnp.sum(jnp.where(here, ia, 0), axis=0, keepdims=True)
        ordered = jnp.sum(jnp.where(here, along, 0), axis=0, keepdims=True)
        previous = jnp.sum(jnp.where(rank == ib - 1, along + 1, 0), axis=0, keepdims=True) - 1
        upto = jnp.sum(jnp.where(along <= ib, 1, 0), axis=0, keepdims=True)
        count = jnp.sum(jnp.where(along == ib, 1, 0), axis=0, keepdims=True)
        last = jnp.maximum(upto - 1, 0)
        board[0:1, 0:nt] = perm
        board[1:2, 0:nt] = jnp.where(ordered == previous, 1, 0)
        board[2:3, 0:nt] = last
        board[3:4, 0:nt] = jnp.where(count > 0, 1, 0)
        for j in range(CHAINS - 1):
            end = run * j + run - 1
            spans = (count > 0) & (upto - count <= end) & (last > end)
            board[4 + j:5 + j, 0:nt] = jnp.where(spans, 1, 0)
        copy = pltpu.make_async_copy(board, table, tsem)
        copy.start()

        def turn(c, carry):
            for i in range(3):
                flip[c, :, i * 128:(i + 1) * 128] = t_ref[c, i * 128:(i + 1) * 128, :].T
            return carry

        lax.fori_loop(0, nb, turn, 0)
        copy.wait()

    def turned():
        order = arrange(gx, gy)

        def one(b, carry):
            q = hbuf[:, b].astype(F32) * scl[...]
            u = q.reshape(nmb * MB, 128).astype(BF16)
            moved = lax.dot_general(order, u, (((1,), (1,)), ((), ())), preferred_element_type=F32)
            ut_ref[b] = moved.astype(BF16)
            return carry

        lax.fori_loop(0, nb, one, 0)

    def forward(k, carry):
        @pl.when(first)
        def _():
            hbuf[k] = x_ref[k]

        @pl.when(sec > 0)
        def _():
            fwhole(k).wait_recv()

        total = jnp.zeros((MB, 128), F32)
        for b in range(nb):
            h = hbuf[k, b]
            hf = h.astype(F32)
            total = total + hf * hf
            hw[b] = h
        mean = jnp.sum(total, axis=1, keepdims=True) * (1.0 / width)
        scale = jnp.broadcast_to(lax.rsqrt(mean + EPS), (MB, 128))
        scl[k] = scale
        for c in range(nb):
            left = jnp.concatenate([hw[rows_ref[3 * c + i]] for i in range(3)], axis=1)
            z = jnp.dot(left, t_ref[c], preferred_element_type=F32)
            a = jnp.tanh(z * scale)
            act[k, c] = 1.0 - a * a
            fout[k, c] = (hbuf[k, c].astype(F32) + a).astype(BF16)
            if (c + 1) % per == 0:
                @pl.when(sec < sections - 1)
                def _(j=c // per):
                    fcopy(k, j).start()
        return carry

    def backward(k, carry):
        @pl.when(final)
        def _():
            gbuf[k] = og_ref[k]

        @pl.when(sec < sections - 1)
        def _():
            bwhole(k).wait_recv()

        for c in range(nb):
            dz = (gbuf[k, c].astype(F32) * act[k, c]).astype(BF16)
            dz_ref[k, c] = dz
            back = jnp.dot(dz, flip[c], preferred_element_type=F32)
            for i in range(3):
                prod[3 * c + i] = back[:, i * 128:(i + 1) * 128]
        scale = scl[k]
        for j in range(CHAINS):
            acc = prod[table[0, run * j]]
            pref[run * j] = acc
            for i in range(run * j + 1, run * j + run):
                acc = acc * table[1, i].astype(F32) + prod[table[0, i]]
                pref[i] = acc
        inner = jnp.zeros((MB, 128), F32)
        for b in range(nb):
            q = hbuf[k, b].astype(F32) * scale
            v = pref[table[2, b]] * table[3, b].astype(F32)
            for j in range(CHAINS - 1):
                v = v + pref[run * j + run - 1] * table[4 + j, b].astype(F32)
            inner = inner + v * q
            prod[b] = v
        inner = jnp.sum(inner, axis=1, keepdims=True) * (1.0 / width)
        inner = jnp.broadcast_to(inner, (MB, 128))
        for b in range(nb):
            q = hbuf[k, b].astype(F32) * scale
            g = gbuf[k, b].astype(F32) + scale * (prod[b] - q * inner)
            gout[k, b] = g.astype(BF16)
            if (b + 1) % per == 0:
                @pl.when(sec > 0)
                def _(j=b // per):
                    bcopy(k, j).start()
        return carry

    early = sec >= sections // 2
    warm = jnp.minimum(1 + AHEAD * (sections - 1 - sec), nmb)

    @pl.when(early)
    def _():
        setup()

    lax.fori_loop(0, warm, forward, 0)

    @pl.when(jnp.logical_not(early))
    def _():
        setup()
        turned()

    def both(k, carry):
        backward(k, carry)
        forward(k + warm, carry)
        return carry

    lax.fori_loop(0, nmb - warm, both, 0)
    lax.fori_loop(nmb - warm, nmb, backward, 0)

    @pl.when(early)
    def _():
        turned()

    def drain(k, carry):
        @pl.when(sec < sections - 1)
        def _():
            fwhole(k).wait_send()

        @pl.when(sec > 0)
        def _():
            bwhole(k).wait_send()

        return carry

    lax.fori_loop(0, nmb, drain, 0)


def reduce_kernel(gx, gy, nb, nmb, rows_ref, ut_ref, dz_ref, out_ref,
                  dzl, own, other, got0, so, sr, sl, ro, got1, sy, got2,
                  s0, r0, s1, r1, s2, r2):
    nt = 3 * nb
    ni = 128 // (2 * gx * gy)
    rx = gy * ni
    per = nt // GROUPS
    half = per // 2
    sub = per // 8
    dp = lax.axis_index("dp")
    me_c = lax.rem(dp, 2)
    me_x = lax.rem(dp // 2, gx)
    me_y = dp // (2 * gx)

    def at(y, x, c):
        return {"dp": (y * gx + x) * 2 + c}

    x_right = lax.rem(me_x + 1, gx)
    x_left = lax.rem(me_x + gx - 1, gx)
    x_over = lax.rem(me_x + 2, gx)
    mate = at(me_y, me_x, 1 - me_c)
    right = at(me_y, x_right, me_c)
    left = at(me_y, x_left, me_c)
    ys = [at(lax.rem(me_y + j, gy), me_x, me_c) for j in range(1, gy)]

    barrier = pltpu.get_barrier_semaphore()
    for peer in [mate, right, left] + ys:
        pl.semaphore_signal(barrier, inc=1, device_id=peer, device_id_type=MESH)

    def prepare(b, carry):
        dzl[b] = dz_ref[:, b].astype(F32).reshape(nmb * MB, 128).astype(BF16)
        return carry

    lax.fori_loop(0, nb, prepare, 0)
    pl.semaphore_wait(barrier, gy + 2)

    def copy0(g):
        return pltpu.make_async_remote_copy(
            src_ref=other.at[g], dst_ref=got0.at[g], send_sem=s0.at[g], recv_sem=r0.at[g],
            device_id=mate, device_id_type=MESH,
        )

    low, high = pl.ds(0, half), pl.ds(half, half)

    def copy1(g, kind):
        src, dst, peer = (
            (so.at[g, low], ro.at[g, 0], right),
            (so.at[g, high], ro.at[g, 1], left),
            (sr.at[g, high], got1.at[g, 0, high], right),
            (sl.at[g, low], got1.at[g, 1, low], left),
            (sr.at[g, low], got1.at[g, 0, low], right),
            (sl.at[g, high], got1.at[g, 1, high], left),
        )[kind]
        return pltpu.make_async_remote_copy(
            src_ref=src, dst_ref=dst, send_sem=s1.at[g, kind], recv_sem=r1.at[g, kind],
            device_id=peer, device_id_type=MESH,
        )

    def copy2(g, j):
        return pltpu.make_async_remote_copy(
            src_ref=sy.at[g, lax.rem(me_y + j, gy)], dst_ref=got2.at[g, j - 1],
            send_sem=s2.at[g, j - 1], recv_sem=r2.at[g, j - 1],
            device_id=ys[j - 1], device_id_type=MESH,
        )

    for g in range(GROUPS):
        def column(c, carry, g=g):
            col = g * (per // 3) + c
            d = dzl[col]
            for i in range(3):
                full = jnp.dot(ut_ref[rows_ref[3 * col + i]], d, preferred_element_type=F32)
                for x in range(gx):
                    own[g, x, 3 * c + i] = full[x * rx:(x + 1) * rx]
                    other[g, x, 3 * c + i] = full[64 + x * rx:64 + (x + 1) * rx].astype(BF16)
            return carry

        lax.fori_loop(0, per // 3, column, 0)
        copy0(g).start()

    def both(g, x, t):
        return own[g, x, t] + got0[g, x, t].astype(F32)

    for g in range(GROUPS):
        copy0(g).wait_recv()

        def over(t, carry, g=g):
            so[g, t] = both(g, x_over, t).astype(BF16)
            return carry

        def straight(t, carry, g=g):
            sr[g, half + t] = both(g, x_right, half + t).astype(BF16)
            sl[g, t] = both(g, x_left, t).astype(BF16)
            return carry

        lax.fori_loop(0, per, over, 0, unroll=4)
        copy1(g, 0).start()
        copy1(g, 1).start()
        lax.fori_loop(0, half, straight, 0, unroll=4)
        copy1(g, 2).start()
        copy1(g, 3).start()

    for g in range(GROUPS):
        copy1(g, 0).wait_recv()
        copy1(g, 1).wait_recv()

        def carried(t, carry, g=g):
            sr[g, t] = (both(g, x_right, t) + ro[g, 0, t].astype(F32)).astype(BF16)
            sl[g, half + t] = (both(g, x_left, half + t) + ro[g, 1, t].astype(F32)).astype(BF16)
            return carry

        lax.fori_loop(0, half, carried, 0, unroll=4)
        copy1(g, 4).start()
        copy1(g, 5).start()

    a = lax.broadcasted_iota(jnp.int32, (8 * rx, 8 * rx), 0)
    b = lax.broadcasted_iota(jnp.int32, (8 * rx, 8 * rx), 1)
    src = lax.rem(a, 8) * rx + (a // (8 * ni)) * ni + lax.rem(a // 8, ni)
    mix = jnp.where(b == src, 1.0, 0.0).astype(BF16)

    for g in range(GROUPS):
        for kind in range(2, 6):
            copy1(g, kind).wait_recv()

        def block(q, carry, g=g):
            pieces = []
            for t in range(8):
                s = both(g, me_x, q * 8 + t)
                for j in range(2):
                    s = s + got1[g, j, q * 8 + t].astype(F32)
                pieces.append(s)
            s = jnp.concatenate(pieces, axis=0).astype(BF16)
            moved = jnp.dot(mix, s, preferred_element_type=F32).astype(BF16)
            for y in range(gy):
                sy[g, y, q] = moved[y * 8 * ni:(y + 1) * 8 * ni]
            return carry

        lax.fori_loop(0, sub, block, 0)
        for j in range(1, gy):
            copy2(g, j).start()

    for g in range(GROUPS):
        for j in range(1, gy):
            copy2(g, j).wait_recv()
        for q in range(sub):
            s = sy[g, me_y, q].astype(F32)
            for j in range(gy - 1):
                s = s + got2[g, j, q].astype(F32)
            for i in range(ni):
                out_ref[i, (g * sub + q) * 8:(g * sub + q + 1) * 8, :] = s[i * 8:(i + 1) * 8]

    for g in range(GROUPS):
        copy0(g).wait_send()
        for kind in range(6):
            copy1(g, kind).wait_send()
        for j in range(1, gy):
            copy2(g, j).wait_send()


def local(gx, gy, inputs, tiles, tile_rows, out_grad):
    sections = lax.axis_size("section")
    rows = tile_rows[0]
    total, width = inputs.shape
    nb = width // 128
    nt = tiles.shape[1]
    nmb = total // MB
    feed = inputs.reshape(nmb, MB, nb, 128).transpose(0, 2, 1, 3)
    seeds = out_grad.reshape(nmb, MB, nb, 128).transpose(0, 2, 1, 3)
    tall = tiles.reshape(nb, 3 * 128, 128)
    smem = pl.BlockSpec(memory_space=pltpu.SMEM)
    vmem = pl.BlockSpec(memory_space=pltpu.VMEM)
    dma = pltpu.SemaphoreType.DMA
    piece = (nmb, nb, MB, 128)
    ut, dz = pl.pallas_call(
        functools.partial(relay_kernel, sections, nmb, nb, gx, gy),
        out_shape=[jax.ShapeDtypeStruct((nb, 128, nmb * MB), BF16), jax.ShapeDtypeStruct(piece, BF16)],
        in_specs=[smem] + [vmem] * 4,
        out_specs=[vmem] * 2,
        scratch_shapes=[
            pltpu.VMEM(piece, BF16), pltpu.VMEM(piece, BF16), pltpu.VMEM(piece, BF16), pltpu.VMEM(piece, BF16),
            pltpu.VMEM((nb, MB, 128), BF16),
            pltpu.VMEM(piece, F32),
            pltpu.VMEM((nmb, MB, 128), F32),
            pltpu.VMEM((nt, MB, 128), F32),
            pltpu.VMEM((nt, MB, 128), F32),
            pltpu.VMEM((nb, 128, 3 * 128), BF16),
            pltpu.VMEM((8, 128), jnp.int32),
            pltpu.SMEM((8, 128), jnp.int32),
            dma(()),
            dma((nmb,)), dma((nmb,)), dma((nmb,)), dma((nmb,)),
        ],
        compiler_params=pltpu.CompilerParams(collective_id=0, has_side_effects=True),
        name="relay",
    )(rows, tile_rows, feed, tall, seeds)
    ni = 128 // (2 * gx * gy)
    rx = gy * ni
    per = nt // GROUPS
    return pl.pallas_call(
        functools.partial(reduce_kernel, gx, gy, nb, nmb),
        out_shape=jax.ShapeDtypeStruct((ni, nt, 128), F32),
        in_specs=[smem] + [vmem] * 2,
        out_specs=vmem,
        scratch_shapes=[
            pltpu.VMEM((nb, nmb * MB, 128), BF16),
            pltpu.VMEM((GROUPS, gx, per, rx, 128), F32),
            pltpu.VMEM((GROUPS, gx, per, rx, 128), BF16),
            pltpu.VMEM((GROUPS, gx, per, rx, 128), BF16),
            pltpu.VMEM((GROUPS, per, rx, 128), BF16),
            pltpu.VMEM((GROUPS, per, rx, 128), BF16),
            pltpu.VMEM((GROUPS, per, rx, 128), BF16),
            pltpu.VMEM((GROUPS, 2, per // 2, rx, 128), BF16),
            pltpu.VMEM((GROUPS, 2, per, rx, 128), BF16),
            pltpu.VMEM((GROUPS, gy, per // 8, 8 * ni, 128), BF16),
            pltpu.VMEM((GROUPS, gy - 1, per // 8, 8 * ni, 128), BF16),
            dma((GROUPS,)), dma((GROUPS,)),
            dma((GROUPS, 6)), dma((GROUPS, 6)),
            dma((GROUPS, gy - 1)), dma((GROUPS, gy - 1)),
        ],
        compiler_params=pltpu.CompilerParams(collective_id=1, has_side_effects=True),
        name="reduce",
    )(rows, ut, dz).reshape(ni, 1, nt, 128)


def solution(mesh, gx=GRID_X, gy=GRID_Y):
    return jax.shard_map(
        functools.partial(local, gx, gy),
        mesh=mesh,
        in_specs=(P("dp", None), P("section", None, None, None), P("section", None), P("dp", None)),
        out_specs=P("dp", "section", None, None),
        check_vma=False,
    )
```

```python
import functools

import jax
import jax.numpy as jnp
from jax import lax
from jax.experimental import pallas as pl
from jax.experimental.pallas import tpu as pltpu
from jax.sharding import PartitionSpec as P

EPS = 1e-06
MB = 8
CHUNKS = 2
CHAINS = 2
AHEAD = 6
GRID_X = 4
GRID_Y = 8
GROUPS = 3
MESH = pl.DeviceIdType.MESH
F32 = jnp.float32
BF16 = jnp.bfloat16


def arrange(gx, gy):
    ni = 128 // (2 * gx * gy)
    rx = gy * ni
    side = lax.rem(lax.axis_index("dp"), 2)
    p = lax.broadcasted_iota(jnp.int32, (128, 128), 0)
    r = lax.broadcasted_iota(jnp.int32, (128, 128), 1)
    far = p // 64
    core = far + side - 2 * far * side
    px = lax.rem(p // rx, gx)
    py = lax.rem(p // ni, gy)
    want = ((py * gx + px) * 2 + core) * ni + lax.rem(p, ni)
    return jnp.where(r == want, 1.0, 0.0).astype(BF16)


def relay_kernel(sections, nmb, nb, gx, gy, rows_ref, line_ref, x_ref, t_ref, og_ref,
                 out_ref,
                 dzo, dzg, uto, uts, utg, own, so, sr, sl, ro, got1, sy, got2,
                 hbuf, gbuf, fout, gout, hw, act, scl, prod, pref, flip, board, table, tsem,
                 fsend, frecv, bsend, brecv, dsend, drecv, us, ur, s1, r1, s2, r2):
    sec = lax.axis_index("section")
    nt = 3 * nb
    width = nb * 128
    per = nb // CHUNKS
    run = nt // CHAINS
    first = sec == 0
    final = sec == sections - 1
    dp = lax.axis_index("dp")
    swap = dp + 1 - 2 * lax.rem(dp, 2)
    straight = sections - 1 - lax.rem(sections - 1, 2)
    up = {"dp": jnp.where(sec < straight, swap, dp), "section": jnp.minimum(sec + 1, sections - 1)}
    down = {"dp": jnp.where(sec - 1 < straight, swap, dp), "section": jnp.maximum(sec - 1, 0)}

    ni = 128 // (2 * gx * gy)
    rx = gy * ni
    tper = nt // GROUPS
    half = tper // 2
    sub = tper // 8
    me_c = lax.rem(dp, 2)
    me_x = lax.rem(dp // 2, gx)
    me_y = dp // (2 * gx)

    def at(y, x):
        return {"dp": (y * gx + x) * 2 + me_c}

    x_right = lax.rem(me_x + 1, gx)
    x_left = lax.rem(me_x + gx - 1, gx)
    x_over = lax.rem(me_x + 2, gx)
    mate = {"dp": swap}
    right = at(me_y, x_right)
    left = at(me_y, x_left)
    ys = [at(lax.rem(me_y + j, gy), me_x) for j in range(1, gy)]

    barrier = pltpu.get_barrier_semaphore()

    @pl.when(sec > 0)
    def _():
        pl.semaphore_signal(barrier, inc=1, device_id=down, device_id_type=MESH)

    @pl.when(sec < sections - 1)
    def _():
        pl.semaphore_signal(barrier, inc=1, device_id=up, device_id_type=MESH)

    for peer in ys + [left, right, mate]:
        pl.semaphore_signal(barrier, inc=1, device_id=peer, device_id_type=MESH)

    pl.semaphore_wait(barrier, gy + 2 + jnp.where(first, 0, 1) + jnp.where(final, 0, 1))

    def fcopy(k, j):
        return pltpu.make_async_remote_copy(
            src_ref=fout.at[k, pl.ds(j * per, per)],
            dst_ref=hbuf.at[k, pl.ds(j * per, per)],
            send_sem=fsend.at[k],
            recv_sem=frecv.at[k],
            device_id=up,
            device_id_type=MESH,
        )

    def bcopy(k, j):
        return pltpu.make_async_remote_copy(
            src_ref=gout.at[k, pl.ds(j * per, per)],
            dst_ref=gbuf.at[k, pl.ds(j * per, per)],
            send_sem=bsend.at[k],
            recv_sem=brecv.at[k],
            device_id=down,
            device_id_type=MESH,
        )

    def fwhole(k):
        return pltpu.make_async_remote_copy(
            src_ref=fout.at[k], dst_ref=hbuf.at[k], send_sem=fsend.at[k], recv_sem=frecv.at[k],
            device_id=up, device_id_type=MESH,
        )

    def bwhole(k):
        return pltpu.make_async_remote_copy(
            src_ref=gout.at[k], dst_ref=gbuf.at[k], send_sem=bsend.at[k], recv_sem=brecv.at[k],
            device_id=down, device_id_type=MESH,
        )

    def dcopy(k):
        return pltpu.make_async_remote_copy(
            src_ref=dzo.at[k], dst_ref=dzg.at[k], send_sem=dsend.at[k], recv_sem=drecv.at[k],
            device_id=mate, device_id_type=MESH,
        )

    def ucopy():
        return pltpu.make_async_remote_copy(
            src_ref=uts, dst_ref=utg, send_sem=us, recv_sem=ur, device_id=mate, device_id_type=MESH,
        )

    def setup():
        ia = lax.broadcasted_iota(jnp.int32, (nt, nt), 0)
        ib = lax.broadcasted_iota(jnp.int32, (nt, nt), 1)
        across = jnp.broadcast_to(line_ref[...], (nt, nt))
        down_col = jnp.sum(jnp.where(ia == ib, across, 0), axis=1, keepdims=True)
        along = jnp.broadcast_to(down_col, (nt, nt))
        ahead = (across < along) | ((across == along) & (ib < ia))
        rank = jnp.broadcast_to(jnp.sum(jnp.where(ahead, 1, 0), axis=1, keepdims=True), (nt, nt))
        here = rank == ib
        perm = jnp.sum(jnp.where(here, ia, 0), axis=0, keepdims=True)
        ordered = jnp.sum(jnp.where(here, along, 0), axis=0, keepdims=True)
        previous = jnp.sum(jnp.where(rank == ib - 1, along + 1, 0), axis=0, keepdims=True) - 1
        upto = jnp.sum(jnp.where(along <= ib, 1, 0), axis=0, keepdims=True)
        count = jnp.sum(jnp.where(along == ib, 1, 0), axis=0, keepdims=True)
        last = jnp.maximum(upto - 1, 0)
        board[0:1, 0:nt] = perm
        board[1:2, 0:nt] = jnp.where(ordered == previous, 1, 0)
        board[2:3, 0:nt] = last
        board[3:4, 0:nt] = jnp.where(count > 0, 1, 0)
        for j in range(CHAINS - 1):
            end = run * j + run - 1
            spans = (count > 0) & (upto - count <= end) & (last > end)
            board[4 + j:5 + j, 0:nt] = jnp.where(spans, 1, 0)
        copy = pltpu.make_async_copy(board, table, tsem)
        copy.start()

        def turn(c, carry):
            for i in range(3):
                flip[c, :, i * 128:(i + 1) * 128] = t_ref[c, i * 128:(i + 1) * 128, :].T
            return carry

        lax.fori_loop(0, nb, turn, 0)
        copy.wait()

    def turned():
        order = arrange(gx, gy)

        def one(b, carry):
            q = hbuf[:, b].astype(F32) * scl[...]
            u = q.reshape(nmb * MB, 128).astype(BF16)
            moved = lax.dot_general(order, u, (((1,), (1,)), ((), ())), preferred_element_type=F32)
            moved = moved.astype(BF16)
            uto[b] = moved[:64]
            uts[b] = moved[64:]
            return carry

        lax.fori_loop(0, nb, one, 0)
        ucopy().start()

    def forward(k, carry):
        @pl.when(first)
        def _():
            hbuf[k] = x_ref[k]

        @pl.when(sec > 0)
        def _():
            fwhole(k).wait_recv()

        total = jnp.zeros((MB, 128), F32)
        for b in range(nb):
            h = hbuf[k, b]
            hf = h.astype(F32)
            total = total + hf * hf
            hw[b] = h
        mean = jnp.sum(total, axis=1, keepdims=True) * (1.0 / width)
        scale = jnp.broadcast_to(lax.rsqrt(mean + EPS), (MB, 128))
        scl[k] = scale
        for c in range(nb):
            left = jnp.concatenate([hw[rows_ref[3 * c + i]] for i in range(3)], axis=1)
            z = jnp.dot(left, t_ref[c], preferred_element_type=F32)
            a = jnp.tanh(z * scale)
            act[k, c] = 1.0 - a * a
            fout[k, c] = (hbuf[k, c].astype(F32) + a).astype(BF16)
            if (c + 1) % per == 0:
                @pl.when(sec < sections - 1)
                def _(j=c // per):
                    fcopy(k, j).start()
        return carry

    def ending(k, carry):
        bwhole(k).wait_recv()
        for c in range(nb):
            dzo[k, c] = (gbuf[k, c].astype(F32) * act[k, c]).astype(BF16)
        dcopy(k).start()
        return carry

    def backward(k, carry):
        @pl.when(final)
        def _():
            gbuf[k] = og_ref[k]

        @pl.when(sec < sections - 1)
        def _():
            bwhole(k).wait_recv()

        for c in range(nb):
            dz = (gbuf[k, c].astype(F32) * act[k, c]).astype(BF16)
            dzo[k, c] = dz
            back = jnp.dot(dz, flip[c], preferred_element_type=F32)
            for i in range(3):
                prod[3 * c + i] = back[:, i * 128:(i + 1) * 128]
        scale = scl[k]
        for j in range(CHAINS):
            acc = prod[table[0, run * j]]
            pref[run * j] = acc
            for i in range(run * j + 1, run * j + run):
                acc = acc * table[1, i].astype(F32) + prod[table[0, i]]
                pref[i] = acc
        inner = jnp.zeros((MB, 128), F32)
        for b in range(nb):
            q = hbuf[k, b].astype(F32) * scale
            v = pref[table[2, b]] * table[3, b].astype(F32)
            for j in range(CHAINS - 1):
                v = v + pref[run * j + run - 1] * table[4 + j, b].astype(F32)
            inner = inner + v * q
            prod[b] = v
        inner = jnp.sum(inner, axis=1, keepdims=True) * (1.0 / width)
        inner = jnp.broadcast_to(inner, (MB, 128))
        for b in range(nb):
            q = hbuf[k, b].astype(F32) * scale
            g = gbuf[k, b].astype(F32) + scale * (prod[b] - q * inner)
            gout[k, b] = g.astype(BF16)
            if (b + 1) % per == 0:
                bcopy(k, b // per).start()
        dcopy(k).start()
        return carry

    early = sec >= sections // 2
    warm = jnp.minimum(1 + AHEAD * (sections - 1 - sec), nmb)

    @pl.when(early)
    def _():
        setup()

    lax.fori_loop(0, warm, forward, 0)

    @pl.when(jnp.logical_not(early))
    def _():
        setup()
        turned()

    def both(k, carry):
        backward(k, carry)
        forward(k + warm, carry)
        return carry

    lax.fori_loop(0, nmb - warm, both, 0)

    @pl.when(sec > 0)
    def _():
        lax.fori_loop(nmb - warm, nmb, backward, 0)

    @pl.when(first)
    def _():
        lax.fori_loop(0, nmb, ending, 0)

    @pl.when(early)
    def _():
        turned()

    ucopy().wait_recv()

    def arrived(k, carry):
        dcopy(k).wait_recv()
        return carry

    lax.fori_loop(0, nmb, arrived, 0)

    low, high = pl.ds(0, half), pl.ds(half, half)

    def copy1(g, kind):
        src, dst, peer = (
            (so.at[g, low], ro.at[g, 0], right),
            (so.at[g, high], ro.at[g, 1], left),
            (sr.at[g, high], got1.at[g, 0, high], right),
            (sl.at[g, low], got1.at[g, 1, low], left),
            (sr.at[g, low], got1.at[g, 0, low], right),
            (sl.at[g, high], got1.at[g, 1, high], left),
        )[kind]
        return pltpu.make_async_remote_copy(
            src_ref=src, dst_ref=dst, send_sem=s1.at[g, kind], recv_sem=r1.at[g, kind],
            device_id=peer, device_id_type=MESH,
        )

    def copy2(g, j):
        return pltpu.make_async_remote_copy(
            src_ref=sy.at[g, lax.rem(me_y + j, gy)], dst_ref=got2.at[g, j - 1],
            send_sem=s2.at[g, j - 1], recv_sem=r2.at[g, j - 1],
            device_id=ys[j - 1], device_id_type=MESH,
        )

    for g in range(GROUPS):
        def column(c, carry, g=g):
            col = g * (tper // 3) + c
            mine = dzo[:, col].astype(F32).reshape(nmb * MB, 128)
            theirs = dzg[:, col].astype(F32).reshape(nmb * MB, 128)
            d = jnp.concatenate([mine, theirs], axis=0).astype(BF16)
            for i in range(3):
                row = rows_ref[3 * col + i]
                wide = jnp.concatenate([uto[row], utg[row]], axis=1)
                full = jnp.dot(wide, d, preferred_element_type=F32)
                for x in range(gx):
                    own[g, x, 3 * c + i] = full[x * rx:(x + 1) * rx]
            return carry

        lax.fori_loop(0, tper // 3, column, 0)

        def over(t, carry, g=g):
            so[g, t] = own[g, x_over, t].astype(BF16)
            return carry

        def straight(t, carry, g=g):
            sr[g, half + t] = own[g, x_right, half + t].astype(BF16)
            sl[g, t] = own[g, x_left, t].astype(BF16)
            return carry

        lax.fori_loop(0, tper, over, 0, unroll=4)
        copy1(g, 0).start()
        copy1(g, 1).start()
        lax.fori_loop(0, half, straight, 0, unroll=4)
        copy1(g, 2).start()
        copy1(g, 3).start()

    for g in range(GROUPS):
        copy1(g, 0).wait_recv()
        copy1(g, 1).wait_recv()

        def carried(t, carry, g=g):
            sr[g, t] = (own[g, x_right, t] + ro[g, 0, t].astype(F32)).astype(BF16)
            sl[g, half + t] = (own[g, x_left, half + t] + ro[g, 1, t].astype(F32)).astype(BF16)
            return carry

        lax.fori_loop(0, half, carried, 0, unroll=4)
        copy1(g, 4).start()
        copy1(g, 5).start()

    a = lax.broadcasted_iota(jnp.int32, (8 * rx, 8 * rx), 0)
    b = lax.broadcasted_iota(jnp.int32, (8 * rx, 8 * rx), 1)
    src = lax.rem(a, 8) * rx + (a // (8 * ni)) * ni + lax.rem(a // 8, ni)
    mix = jnp.where(b == src, 1.0, 0.0).astype(BF16)

    for g in range(GROUPS):
        for kind in range(2, 6):
            copy1(g, kind).wait_recv()

        def block(q, carry, g=g):
            pieces = []
            for t in range(8):
                s = own[g, me_x, q * 8 + t]
                for j in range(2):
                    s = s + got1[g, j, q * 8 + t].astype(F32)
                pieces.append(s)
            s = jnp.concatenate(pieces, axis=0).astype(BF16)
            moved = jnp.dot(mix, s, preferred_element_type=F32).astype(BF16)
            for y in range(gy):
                sy[g, y, q] = moved[y * 8 * ni:(y + 1) * 8 * ni]
            return carry

        lax.fori_loop(0, sub, block, 0)
        for j in range(1, gy):
            copy2(g, j).start()

    for g in range(GROUPS):
        for j in range(1, gy):
            copy2(g, j).wait_recv()
        for q in range(sub):
            s = sy[g, me_y, q].astype(F32)
            for j in range(gy - 1):
                s = s + got2[g, j, q].astype(F32)
            for i in range(ni):
                out_ref[i, (g * sub + q) * 8:(g * sub + q + 1) * 8, :] = s[i * 8:(i + 1) * 8]

    for g in range(GROUPS):
        for kind in range(6):
            copy1(g, kind).wait_send()
        for j in range(1, gy):
            copy2(g, j).wait_send()
    ucopy().wait_send()

    def drain(k, carry):
        @pl.when(sec < sections - 1)
        def _():
            fwhole(k).wait_send()

        @pl.when(sec > 0)
        def _():
            bwhole(k).wait_send()

        dcopy(k).wait_send()
        return carry

    lax.fori_loop(0, nmb, drain, 0)


def local(gx, gy, inputs, tiles, tile_rows, out_grad):
    sections = lax.axis_size("section")
    rows = tile_rows[0]
    total, width = inputs.shape
    nb = width // 128
    nt = tiles.shape[1]
    nmb = total // MB
    feed = inputs.reshape(nmb, MB, nb, 128).transpose(0, 2, 1, 3)
    seeds = out_grad.reshape(nmb, MB, nb, 128).transpose(0, 2, 1, 3)
    tall = tiles.reshape(nb, 3 * 128, 128)
    smem = pl.BlockSpec(memory_space=pltpu.SMEM)
    vmem = pl.BlockSpec(memory_space=pltpu.VMEM)
    dma = pltpu.SemaphoreType.DMA
    piece = (nmb, nb, MB, 128)
    ni = 128 // (2 * gx * gy)
    rx = gy * ni
    tper = nt // GROUPS
    strip = (nb, 64, nmb * MB)
    return pl.pallas_call(
        functools.partial(relay_kernel, sections, nmb, nb, gx, gy),
        out_shape=jax.ShapeDtypeStruct((ni, nt, 128), F32),
        in_specs=[smem] + [vmem] * 4,
        out_specs=vmem,
        scratch_shapes=[
            pltpu.VMEM(piece, BF16), pltpu.VMEM(piece, BF16),
            pltpu.VMEM(strip, BF16), pltpu.VMEM(strip, BF16), pltpu.VMEM(strip, BF16),
            pltpu.VMEM((GROUPS, gx, tper, rx, 128), F32),
            pltpu.VMEM((GROUPS, tper, rx, 128), BF16),
            pltpu.VMEM((GROUPS, tper, rx, 128), BF16),
            pltpu.VMEM((GROUPS, tper, rx, 128), BF16),
            pltpu.VMEM((GROUPS, 2, tper // 2, rx, 128), BF16),
            pltpu.VMEM((GROUPS, 2, tper, rx, 128), BF16),
            pltpu.VMEM((GROUPS, gy, tper // 8, 8 * ni, 128), BF16),
            pltpu.VMEM((GROUPS, gy - 1, tper // 8, 8 * ni, 128), BF16),
            pltpu.VMEM(piece, BF16), pltpu.VMEM(piece, BF16), pltpu.VMEM(piece, BF16), pltpu.VMEM(piece, BF16),
            pltpu.VMEM((nb, MB, 128), BF16),
            pltpu.VMEM(piece, F32),
            pltpu.VMEM((nmb, MB, 128), F32),
            pltpu.VMEM((nt, MB, 128), F32),
            pltpu.VMEM((nt, MB, 128), F32),
            pltpu.VMEM((nb, 128, 3 * 128), BF16),
            pltpu.VMEM((8, 128), jnp.int32),
            pltpu.SMEM((8, 128), jnp.int32),
            dma(()),
            dma((nmb,)), dma((nmb,)), dma((nmb,)), dma((nmb,)), dma((nmb,)), dma((nmb,)),
            dma(()), dma(()),
            dma((GROUPS, 6)), dma((GROUPS, 6)),
            dma((GROUPS, gy - 1)), dma((GROUPS, gy - 1)),
        ],
        compiler_params=pltpu.CompilerParams(collective_id=0, has_side_effects=True),
        name="relay",
    )(rows, tile_rows, feed, tall, seeds).reshape(ni, 1, nt, 128)


def solution(mesh, gx=GRID_X, gy=GRID_Y):
    return jax.shard_map(
        functools.partial(local, gx, gy),
        mesh=mesh,
        in_specs=(P("dp", None), P("section", None, None, None), P("section", None), P("dp", None)),
        out_specs=P("dp", "section", None, None),
        check_vma=False,
    )
```

```python
import functools

import jax
import jax.numpy as jnp
from jax import lax
from jax.experimental import pallas as pl
from jax.experimental.pallas import tpu as pltpu
from jax.sharding import PartitionSpec as P

EPS = 1e-06
MB = 8
CHUNKS = 2
CHAINS = 2
AHEAD = 6
LAG = 4
GRID_X = 4
GRID_Y = 8
GROUPS = 3
MESH = pl.DeviceIdType.MESH
F32 = jnp.float32
BF16 = jnp.bfloat16


def arrange(gx, gy):
    ni = 128 // (2 * gx * gy)
    rx = gy * ni
    side = lax.rem(lax.axis_index("dp"), 2)
    p = lax.broadcasted_iota(jnp.int32, (128, 128), 0)
    r = lax.broadcasted_iota(jnp.int32, (128, 128), 1)
    far = p // 64
    core = far + side - 2 * far * side
    px = lax.rem(p // rx, gx)
    py = lax.rem(p // ni, gy)
    want = ((py * gx + px) * 2 + core) * ni + lax.rem(p, ni)
    return jnp.where(r == want, 1.0, 0.0).astype(BF16)


def relay_kernel(sections, nmb, nb, gx, gy, rows_ref, line_ref, x_ref, t_ref, og_ref,
                 out_ref,
                 dzb, ub, uts, own, so, sr, sl, ro, got1, sy, got2,
                 hbuf, gbuf, fout, gout, hw, act, scl, prod, pref, flip, board, table, tsem,
                 fsend, frecv, bsend, brecv, dsend, drecv, us, ur, s1, r1, s2, r2, xsend, xrecv, ready):
    sec = lax.axis_index("section")
    dp = lax.axis_index("dp")
    nt = 3 * nb
    width = nb * 128
    per = nb // CHUNKS
    run = nt // CHAINS
    ni = 128 // (2 * gx * gy)
    rx = gy * ni
    tper = nt // GROUPS
    half = tper // 2
    sub = tper // 8
    me_c = lax.rem(dp, 2)
    me_x = lax.rem(dp // 2, gx)
    me_y = dp // (2 * gx)
    first = sec == 0
    final = sec == sections - 1
    odd = me_c == 1
    worker = first & odd
    idle = first & jnp.logical_not(odd)
    feeder = (sec == 1) & jnp.logical_not(odd)
    swap = dp + 1 - 2 * me_c
    straight = sections - 1 - lax.rem(sections - 1, 2)
    above = jnp.minimum(sec + 1, sections - 1)
    below = jnp.maximum(sec - 1, 0)
    up_dp = jnp.where(sec < straight, swap, dp)
    down_dp = jnp.where(sec == 1, dp + 1 - me_c, jnp.where(sec - 1 < straight, swap, dp))
    offset = jnp.where((sec == 1) & odd, nmb, 0)
    down = {"dp": down_dp, "section": below}
    mate = {"dp": swap}

    def at(y, x):
        return {"dp": (y * gx + x) * 2 + me_c}

    x_right = lax.rem(me_x + 1, gx)
    x_left = lax.rem(me_x + gx - 1, gx)
    x_over = lax.rem(me_x + 2, gx)
    right = at(me_y, x_right)
    left = at(me_y, x_left)
    ys = [at(lax.rem(me_y + j, gy), me_x) for j in range(1, gy)]

    barrier = pltpu.get_barrier_semaphore()

    def greet(peer):
        pl.semaphore_signal(barrier, inc=1, device_id=peer, device_id_type=MESH)

    @pl.when(sec > 0)
    def _():
        greet(down)

    @pl.when((sec > 0) & (sec < sections - 1))
    def _():
        greet({"dp": up_dp, "section": above})

    @pl.when(worker)
    def _():
        greet({"dp": swap, "section": above})
        greet({"dp": dp, "section": above})

    for peer in [left, right] + ys:
        greet(peer)

    @pl.when(jnp.logical_not(idle))
    def _():
        greet(mate)

    count = gy + 1 + jnp.where(first, jnp.where(odd, 2, 1), 2 + jnp.where(final, 0, 1))
    pl.semaphore_wait(barrier, count)

    @pl.when(idle)
    def _():
        pl.semaphore_signal(ready, inc=1, device_id=mate, device_id_type=MESH)

    def xcopy(k):
        return pltpu.make_async_remote_copy(
            src_ref=x_ref.at[k], dst_ref=hbuf.at[nmb + k], send_sem=xsend.at[k], recv_sem=xrecv.at[k],
            device_id={"dp": dp + 1 - me_c, "section": below}, device_id_type=MESH,
        )

    @pl.when(feeder)
    def _():
        def feed(k, carry):
            xcopy(k).start()
            return carry

        lax.fori_loop(0, nmb, feed, 0)

    def target(slot):
        return {"dp": jnp.where(first & (slot >= nmb), dp, up_dp), "section": above}

    def fcopy(slot, j):
        return pltpu.make_async_remote_copy(
            src_ref=fout.at[slot, pl.ds(j * per, per)],
            dst_ref=hbuf.at[lax.rem(slot, nmb), pl.ds(j * per, per)],
            send_sem=fsend.at[slot],
            recv_sem=frecv.at[lax.rem(slot, nmb)],
            device_id=target(slot),
            device_id_type=MESH,
        )

    def bcopy(k, j):
        return pltpu.make_async_remote_copy(
            src_ref=gout.at[k, pl.ds(j * per, per)],
            dst_ref=gbuf.at[k + offset, pl.ds(j * per, per)],
            send_sem=bsend.at[k],
            recv_sem=brecv.at[k + offset],
            device_id=down,
            device_id_type=MESH,
        )

    def fsent(slot):
        pltpu.make_async_remote_copy(
            src_ref=fout.at[slot], dst_ref=hbuf.at[lax.rem(slot, nmb)], send_sem=fsend.at[slot],
            recv_sem=frecv.at[lax.rem(slot, nmb)], device_id=target(slot), device_id_type=MESH,
        ).wait_send()

    def fgot(k):
        pltpu.make_async_remote_copy(
            src_ref=fout.at[k], dst_ref=hbuf.at[k], send_sem=fsend.at[k], recv_sem=frecv.at[k],
            device_id=target(k), device_id_type=MESH,
        ).wait_recv()

    def bsent(k):
        pltpu.make_async_remote_copy(
            src_ref=gout.at[k], dst_ref=gbuf.at[k + offset], send_sem=bsend.at[k], recv_sem=brecv.at[k + offset],
            device_id=down, device_id_type=MESH,
        ).wait_send()

    def bgot(slot):
        pltpu.make_async_remote_copy(
            src_ref=gout.at[lax.rem(slot, nmb)], dst_ref=gbuf.at[slot], send_sem=bsend.at[lax.rem(slot, nmb)],
            recv_sem=brecv.at[slot], device_id=down, device_id_type=MESH,
        ).wait_recv()

    def dcopy(slot):
        place = lax.rem(slot + nmb, 2 * nmb)
        return pltpu.make_async_remote_copy(
            src_ref=dzb.at[slot], dst_ref=dzb.at[place], send_sem=dsend.at[slot], recv_sem=drecv.at[place],
            device_id=mate, device_id_type=MESH,
        )

    def dgot(slot):
        pltpu.make_async_remote_copy(
            src_ref=dzb.at[slot], dst_ref=dzb.at[slot], send_sem=dsend.at[slot], recv_sem=drecv.at[slot],
            device_id=mate, device_id_type=MESH,
        ).wait_recv()

    def ucopy(h):
        return pltpu.make_async_remote_copy(
            src_ref=uts.at[h], dst_ref=ub.at[1 - h], send_sem=us.at[h], recv_sem=ur.at[1 - h],
            device_id=mate, device_id_type=MESH,
        )

    def setup():
        ia = lax.broadcasted_iota(jnp.int32, (nt, nt), 0)
        ib = lax.broadcasted_iota(jnp.int32, (nt, nt), 1)
        across = jnp.broadcast_to(line_ref[...], (nt, nt))
        down_col = jnp.sum(jnp.where(ia == ib, across, 0), axis=1, keepdims=True)
        along = jnp.broadcast_to(down_col, (nt, nt))
        ahead = (across < along) | ((across == along) & (ib < ia))
        rank = jnp.broadcast_to(jnp.sum(jnp.where(ahead, 1, 0), axis=1, keepdims=True), (nt, nt))
        here = rank == ib
        perm = jnp.sum(jnp.where(here, ia, 0), axis=0, keepdims=True)
        ordered = jnp.sum(jnp.where(here, along, 0), axis=0, keepdims=True)
        previous = jnp.sum(jnp.where(rank == ib - 1, along + 1, 0), axis=0, keepdims=True) - 1
        upto = jnp.sum(jnp.where(along <= ib, 1, 0), axis=0, keepdims=True)
        count = jnp.sum(jnp.where(along == ib, 1, 0), axis=0, keepdims=True)
        last = jnp.maximum(upto - 1, 0)
        board[0:1, 0:nt] = perm
        board[1:2, 0:nt] = jnp.where(ordered == previous, 1, 0)
        board[2:3, 0:nt] = last
        board[3:4, 0:nt] = jnp.where(count > 0, 1, 0)
        for j in range(CHAINS - 1):
            end = run * j + run - 1
            spans = (count > 0) & (upto - count <= end) & (last > end)
            board[4 + j:5 + j, 0:nt] = jnp.where(spans, 1, 0)
        copy = pltpu.make_async_copy(board, table, tsem)
        copy.start()

        def turn(c, carry):
            for i in range(3):
                flip[c, :, i * 128:(i + 1) * 128] = t_ref[c, i * 128:(i + 1) * 128, :].T
            return carry

        lax.fori_loop(0, nb, turn, 0)
        copy.wait()

    def turned(h):
        order = arrange(gx, gy)

        def one(b, carry):
            q = hbuf[h * nmb:(h + 1) * nmb, b].astype(F32) * scl[h * nmb:(h + 1) * nmb]
            u = q.reshape(nmb * MB, 128).astype(BF16)
            moved = lax.dot_general(order, u, (((1,), (1,)), ((), ())), preferred_element_type=F32)
            moved = moved.astype(BF16)
            ub[h, b] = moved[:64]
            uts[h, b] = moved[64:]
            return carry

        lax.fori_loop(0, nb, one, 0)
        ucopy(h).start()

    def forward(k, carry):
        @pl.when(first & (k < nmb))
        def _():
            hbuf[k] = x_ref[lax.rem(k, nmb)]

        @pl.when(first & (k >= nmb))
        def _():
            xcopy(k - nmb).wait_recv()

        @pl.when(sec > 0)
        def _():
            fgot(k)

        total = jnp.zeros((MB, 128), F32)
        for b in range(nb):
            h = hbuf[k, b]
            hf = h.astype(F32)
            total = total + hf * hf
            hw[b] = h
        mean = jnp.sum(total, axis=1, keepdims=True) * (1.0 / width)
        scale = jnp.broadcast_to(lax.rsqrt(mean + EPS), (MB, 128))
        scl[k] = scale
        for c in range(nb):
            left = jnp.concatenate([hw[rows_ref[3 * c + i]] for i in range(3)], axis=1)
            z = jnp.dot(left, t_ref[c], preferred_element_type=F32)
            a = jnp.tanh(z * scale)
            act[k, c] = 1.0 - a * a
            fout[k, c] = (hbuf[k, c].astype(F32) + a).astype(BF16)
            if (c + 1) % per == 0:
                @pl.when(sec < sections - 1)
                def _(j=c // per):
                    fcopy(k, j).start()
        return carry

    def ending(k, carry):
        bgot(k)
        for c in range(nb):
            dzb[k, c] = (gbuf[k, c].astype(F32) * act[k, c]).astype(BF16)
        dcopy(k).start()
        return carry

    def backward(k, carry):
        @pl.when(final)
        def _():
            gbuf[k] = og_ref[k]

        @pl.when(sec < sections - 1)
        def _():
            bgot(k)

        for c in range(nb):
            dz = (gbuf[k, c].astype(F32) * act[k, c]).astype(BF16)
            dzb[k, c] = dz
            back = jnp.dot(dz, flip[c], preferred_element_type=F32)
            for i in range(3):
                prod[3 * c + i] = back[:, i * 128:(i + 1) * 128]
        scale = scl[k]
        for j in range(CHAINS):
            acc = prod[table[0, run * j]]
            pref[run * j] = acc
            for i in range(run * j + 1, run * j + run):
                acc = acc * table[1, i].astype(F32) + prod[table[0, i]]
                pref[i] = acc
        inner = jnp.zeros((MB, 128), F32)
        for b in range(nb):
            q = hbuf[k, b].astype(F32) * scale
            v = pref[table[2, b]] * table[3, b].astype(F32)
            for j in range(CHAINS - 1):
                v = v + pref[run * j + run - 1] * table[4 + j, b].astype(F32)
            inner = inner + v * q
            prod[b] = v
        inner = jnp.sum(inner, axis=1, keepdims=True) * (1.0 / width)
        inner = jnp.broadcast_to(inner, (MB, 128))
        for b in range(nb):
            q = hbuf[k, b].astype(F32) * scale
            g = gbuf[k, b].astype(F32) + scale * (prod[b] - q * inner)
            gout[k, b] = g.astype(BF16)
            if (b + 1) % per == 0:
                bcopy(k, b // per).start()
        dcopy(k).start()
        return carry

    early = sec >= sections // 2
    late = jnp.logical_not(early | first)
    warm = jnp.minimum(1 + AHEAD * (sections - 1 - sec), nmb)
    rounds = jnp.where(first, jnp.where(odd, 2 * nmb, 0), warm)
    paired = jnp.where(first, 0, nmb - warm)

    @pl.when(early)
    def _():
        setup()

    def opening(i, carry):
        j = i - LAG
        mixed = jnp.where(lax.rem(j, 2) == 0, nmb + j // 2, LAG + j // 2)
        mixed = jnp.where(i < LAG, i, jnp.where(i >= 2 * nmb - LAG, i, mixed))
        return forward(jnp.where(first, mixed, i), carry)

    lax.fori_loop(0, rounds, opening, 0)

    @pl.when(late)
    def _():
        setup()
        turned(0)

    @pl.when(worker)
    def _():
        pl.semaphore_wait(ready, 1)
        turned(0)
        turned(1)

    def both(k, carry):
        backward(k, carry)
        forward(k + warm, carry)
        return carry

    lax.fori_loop(0, paired, both, 0)

    @pl.when(sec > 0)
    def _():
        lax.fori_loop(nmb - warm, nmb, backward, 0)

    @pl.when(worker)
    def _():
        def alternate(i, carry):
            return ending(i // 2 + nmb * lax.rem(i, 2), carry)

        lax.fori_loop(0, 2 * nmb, alternate, 0)

    @pl.when(early)
    def _():
        turned(0)

    @pl.when(idle)
    def _():
        ucopy(1).wait_recv()

    @pl.when(jnp.logical_not(worker))
    def _():
        ucopy(0).wait_recv()

    def arrived(k, carry):
        dgot(k)
        return carry

    lax.fori_loop(jnp.where(first, jnp.where(odd, 2 * nmb, 0), nmb), 2 * nmb, arrived, 0)

    low, high = pl.ds(0, half), pl.ds(half, half)

    def copy1(g, kind):
        src, dst, peer = (
            (so.at[g, low], ro.at[g, 0], right),
            (so.at[g, high], ro.at[g, 1], left),
            (sr.at[g, high], got1.at[g, 0, high], right),
            (sl.at[g, low], got1.at[g, 1, low], left),
            (sr.at[g, low], got1.at[g, 0, low], right),
            (sl.at[g, high], got1.at[g, 1, high], left),
        )[kind]
        return pltpu.make_async_remote_copy(
            src_ref=src, dst_ref=dst, send_sem=s1.at[g, kind], recv_sem=r1.at[g, kind],
            device_id=peer, device_id_type=MESH,
        )

    def copy2(g, j):
        return pltpu.make_async_remote_copy(
            src_ref=sy.at[g, lax.rem(me_y + j, gy)], dst_ref=got2.at[g, j - 1],
            send_sem=s2.at[g, j - 1], recv_sem=r2.at[g, j - 1],
            device_id=ys[j - 1], device_id_type=MESH,
        )

    for g in range(GROUPS):
        def column(c, carry, g=g):
            col = g * (tper // 3) + c
            d = dzb[:, col].astype(F32).reshape(2 * nmb * MB, 128).astype(BF16)
            for i in range(3):
                row = rows_ref[3 * col + i]
                wide = jnp.concatenate([ub[0, row], ub[1, row]], axis=1)
                full = jnp.dot(wide, d, preferred_element_type=F32)
                for x in range(gx):
                    own[g, x, 3 * c + i] = full[x * rx:(x + 1) * rx]
            return carry

        lax.fori_loop(0, tper // 3, column, 0)

        def over(t, carry, g=g):
            so[g, t] = own[g, x_over, t].astype(BF16)
            return carry

        def straight(t, carry, g=g):
            sr[g, half + t] = own[g, x_right, half + t].astype(BF16)
            sl[g, t] = own[g, x_left, t].astype(BF16)
            return carry

        lax.fori_loop(0, tper, over, 0, unroll=4)
        copy1(g, 0).start()
        copy1(g, 1).start()
        lax.fori_loop(0, half, straight, 0, unroll=4)
        copy1(g, 2).start()
        copy1(g, 3).start()

    for g in range(GROUPS):
        copy1(g, 0).wait_recv()
        copy1(g, 1).wait_recv()

        def carried(t, carry, g=g):
            sr[g, t] = (own[g, x_right, t] + ro[g, 0, t].astype(F32)).astype(BF16)
            sl[g, half + t] = (own[g, x_left, half + t] + ro[g, 1, t].astype(F32)).astype(BF16)
            return carry

        lax.fori_loop(0, half, carried, 0, unroll=4)
        copy1(g, 4).start()
        copy1(g, 5).start()

    a = lax.broadcasted_iota(jnp.int32, (8 * rx, 8 * rx), 0)
    b = lax.broadcasted_iota(jnp.int32, (8 * rx, 8 * rx), 1)
    src = lax.rem(a, 8) * rx + (a // (8 * ni)) * ni + lax.rem(a // 8, ni)
    mix = jnp.where(b == src, 1.0, 0.0).astype(BF16)

    for g in range(GROUPS):
        for kind in range(2, 6):
            copy1(g, kind).wait_recv()

        def block(q, carry, g=g):
            pieces = []
            for t in range(8):
                s = own[g, me_x, q * 8 + t]
                for j in range(2):
                    s = s + got1[g, j, q * 8 + t].astype(F32)
                pieces.append(s)
            s = jnp.concatenate(pieces, axis=0).astype(BF16)
            moved = jnp.dot(mix, s, preferred_element_type=F32).astype(BF16)
            for y in range(gy):
                sy[g, y, q] = moved[y * 8 * ni:(y + 1) * 8 * ni]
            return carry

        lax.fori_loop(0, sub, block, 0)
        for j in range(1, gy):
            copy2(g, j).start()

    for g in range(GROUPS):
        for j in range(1, gy):
            copy2(g, j).wait_recv()
        for q in range(sub):
            s = sy[g, me_y, q].astype(F32)
            for j in range(gy - 1):
                s = s + got2[g, j, q].astype(F32)
            for i in range(ni):
                out_ref[i, (g * sub + q) * 8:(g * sub + q + 1) * 8, :] = s[i * 8:(i + 1) * 8]

    for g in range(GROUPS):
        for kind in range(6):
            copy1(g, kind).wait_send()
        for j in range(1, gy):
            copy2(g, j).wait_send()

    @pl.when(jnp.logical_not(idle))
    def _():
        ucopy(0).wait_send()

    @pl.when(worker)
    def _():
        ucopy(1).wait_send()

    def fdrain(k, carry):
        fsent(k)
        return carry

    def bdrain(k, carry):
        bsent(k)
        return carry

    def ddrain(k, carry):
        dcopy(k).wait_send()
        return carry

    def xdrain(k, carry):
        xcopy(k).wait_send()
        return carry

    sent = jnp.where(first, jnp.where(odd, 2 * nmb, 0), nmb)
    lax.fori_loop(0, jnp.where(final, 0, sent), fdrain, 0)
    lax.fori_loop(0, jnp.where(first, 0, nmb), bdrain, 0)
    lax.fori_loop(0, sent, ddrain, 0)
    lax.fori_loop(0, jnp.where(feeder, nmb, 0), xdrain, 0)


def local(gx, gy, inputs, tiles, tile_rows, out_grad):
    sections = lax.axis_size("section")
    rows = tile_rows[0]
    total, width = inputs.shape
    nb = width // 128
    nt = tiles.shape[1]
    nmb = total // MB
    feed = inputs.reshape(nmb, MB, nb, 128).transpose(0, 2, 1, 3)
    seeds = out_grad.reshape(nmb, MB, nb, 128).transpose(0, 2, 1, 3)
    tall = tiles.reshape(nb, 3 * 128, 128)
    smem = pl.BlockSpec(memory_space=pltpu.SMEM)
    vmem = pl.BlockSpec(memory_space=pltpu.VMEM)
    dma = pltpu.SemaphoreType.DMA
    piece = (nmb, nb, MB, 128)
    ni = 128 // (2 * gx * gy)
    rx = gy * ni
    tper = nt // GROUPS
    strip = (2, nb, 64, nmb * MB)
    twice = (2 * nmb, nb, MB, 128)
    return pl.pallas_call(
        functools.partial(relay_kernel, sections, nmb, nb, gx, gy),
        out_shape=jax.ShapeDtypeStruct((ni, nt, 128), F32),
        in_specs=[smem] + [vmem] * 4,
        out_specs=vmem,
        scratch_shapes=[
            pltpu.VMEM(twice, BF16),
            pltpu.VMEM(strip, BF16), pltpu.VMEM(strip, BF16),
            pltpu.VMEM((GROUPS, gx, tper, rx, 128), F32),
            pltpu.VMEM((GROUPS, tper, rx, 128), BF16),
            pltpu.VMEM((GROUPS, tper, rx, 128), BF16),
            pltpu.VMEM((GROUPS, tper, rx, 128), BF16),
            pltpu.VMEM((GROUPS, 2, tper // 2, rx, 128), BF16),
            pltpu.VMEM((GROUPS, 2, tper, rx, 128), BF16),
            pltpu.VMEM((GROUPS, gy, tper // 8, 8 * ni, 128), BF16),
            pltpu.VMEM((GROUPS, gy - 1, tper // 8, 8 * ni, 128), BF16),
            pltpu.VMEM(twice, BF16), pltpu.VMEM(twice, BF16), pltpu.VMEM(twice, BF16), pltpu.VMEM(piece, BF16),
            pltpu.VMEM((nb, MB, 128), BF16),
            pltpu.VMEM(twice, F32),
            pltpu.VMEM((2 * nmb, MB, 128), F32),
            pltpu.VMEM((nt, MB, 128), F32),
            pltpu.VMEM((nt, MB, 128), F32),
            pltpu.VMEM((nb, 128, 3 * 128), BF16),
            pltpu.VMEM((8, 128), jnp.int32),
            pltpu.SMEM((8, 128), jnp.int32),
            dma(()),
            dma((2 * nmb,)), dma((nmb,)), dma((nmb,)), dma((2 * nmb,)), dma((2 * nmb,)), dma((2 * nmb,)),
            dma((2,)), dma((2,)),
            dma((GROUPS, 6)), dma((GROUPS, 6)),
            dma((GROUPS, gy - 1)), dma((GROUPS, gy - 1)),
            dma((nmb,)), dma((nmb,)), pltpu.SemaphoreType.REGULAR,
        ],
        compiler_params=pltpu.CompilerParams(collective_id=0, has_side_effects=True),
        name="relay",
    )(rows, tile_rows, feed, tall, seeds).reshape(ni, 1, nt, 128)


def solution(mesh, gx=GRID_X, gy=GRID_Y):
    return jax.shard_map(
        functools.partial(local, gx, gy),
        mesh=mesh,
        in_specs=(P("dp", None), P("section", None, None, None), P("section", None), P("dp", None)),
        out_specs=P("dp", "section", None, None),
        check_vma=False,
    )
```

```python
import functools

import jax
import jax.numpy as jnp
from jax import lax
from jax.experimental import pallas as pl
from jax.experimental.pallas import tpu as pltpu
from jax.sharding import PartitionSpec as P

EPS = 1e-06
MB = 8
CHUNKS = 2
CHAINS = 2
AHEAD = 6
LAG = 2
GRID_X = 4
GRID_Y = 8
GROUPS = 3
MESH = pl.DeviceIdType.MESH
F32 = jnp.float32
BF16 = jnp.bfloat16


def arrange(gx, gy):
    ni = 128 // (2 * gx * gy)
    rx = gy * ni
    side = lax.rem(lax.axis_index("dp"), 2)
    p = lax.broadcasted_iota(jnp.int32, (128, 128), 0)
    r = lax.broadcasted_iota(jnp.int32, (128, 128), 1)
    far = p // 64
    core = far + side - 2 * far * side
    px = lax.rem(p // rx, gx)
    py = lax.rem(p // ni, gy)
    want = ((py * gx + px) * 2 + core) * ni + lax.rem(p, ni)
    return jnp.where(r == want, 1.0, 0.0).astype(BF16)


def relay_kernel(sections, nmb, nb, gx, gy, rows_ref, line_ref, x_ref, t_ref, og_ref,
                 out_ref,
                 dzb, ub, uts, own, so, sr, sl, ro, got1, sy, got2,
                 hbuf, gbuf, fout, gout, hw, act, scl, prod, pref, flip, board, table, tsem,
                 fsend, frecv, bsend, brecv, dsend, drecv, us, ur, s1, r1, s2, r2, xsend, xrecv, ready, go):
    sec = lax.axis_index("section")
    dp = lax.axis_index("dp")
    nt = 3 * nb
    width = nb * 128
    per = nb // CHUNKS
    run = nt // CHAINS
    ni = 128 // (2 * gx * gy)
    rx = gy * ni
    tper = nt // GROUPS
    half = tper // 2
    sub = tper // 8
    me_c = lax.rem(dp, 2)
    me_x = lax.rem(dp // 2, gx)
    me_y = dp // (2 * gx)
    first = sec == 0
    final = sec == sections - 1
    odd = me_c == 1
    worker = first & odd
    idle = first & jnp.logical_not(odd)
    feeder = (sec == 1) & jnp.logical_not(odd)
    swap = dp + 1 - 2 * me_c
    straight = sections - 1 - lax.rem(sections - 1, 2)
    above = jnp.minimum(sec + 1, sections - 1)
    below = jnp.maximum(sec - 1, 0)
    up_dp = jnp.where(sec < straight, swap, dp)
    down_dp = jnp.where(sec == 1, dp + 1 - me_c, jnp.where(sec - 1 < straight, swap, dp))
    offset = jnp.where((sec == 1) & odd, nmb, 0)
    down = {"dp": down_dp, "section": below}
    mate = {"dp": swap}

    def at(y, x):
        return {"dp": (y * gx + x) * 2 + me_c}

    x_right = lax.rem(me_x + 1, gx)
    x_left = lax.rem(me_x + gx - 1, gx)
    x_over = lax.rem(me_x + 2, gx)
    right = at(me_y, x_right)
    left = at(me_y, x_left)
    ys = [at(lax.rem(me_y + j, gy), me_x) for j in range(1, gy)]

    barrier = pltpu.get_barrier_semaphore()

    def greet(peer):
        pl.semaphore_signal(barrier, inc=1, device_id=peer, device_id_type=MESH)

    @pl.when(sec > 0)
    def _():
        greet(down)

    @pl.when((sec > 0) & (sec < sections - 1))
    def _():
        greet({"dp": up_dp, "section": above})

    @pl.when(worker)
    def _():
        greet({"dp": swap, "section": above})
        greet({"dp": dp, "section": above})

    for peer in [left, right] + ys:
        greet({"dp": jnp.where(first, peer["dp"] - me_c, peer["dp"])})

    @pl.when(jnp.logical_not(idle))
    def _():
        greet(mate)

    def xcopy(k):
        return pltpu.make_async_remote_copy(
            src_ref=x_ref.at[k], dst_ref=hbuf.at[nmb + k], send_sem=xsend.at[k], recv_sem=xrecv.at[k],
            device_id={"dp": dp + 1 - me_c, "section": below}, device_id_type=MESH,
        )

    @pl.when(worker)
    def _():
        pl.semaphore_wait(barrier, 2)
        pl.semaphore_signal(go, inc=1, device_id={"dp": swap, "section": above}, device_id_type=MESH)

    @pl.when(feeder)
    def _():
        pl.semaphore_wait(go, 1)

        def feed(k, carry):
            xcopy(k).start()
            return carry

        lax.fori_loop(0, nmb, feed, 0)

    @pl.when(jnp.logical_not(worker))
    def _():
        plane = gy + 2 + jnp.where(first, gy + 1, 1 + jnp.where(final, 0, 1))
        pl.semaphore_wait(barrier, plane)

    @pl.when(idle)
    def _():
        pl.semaphore_signal(ready, inc=1, device_id=mate, device_id_type=MESH)

    def target(slot):
        return {"dp": jnp.where(first & (slot >= nmb), dp, up_dp), "section": above}

    def fcopy(slot, j):
        return pltpu.make_async_remote_copy(
            src_ref=fout.at[slot, pl.ds(j * per, per)],
            dst_ref=hbuf.at[lax.rem(slot, nmb), pl.ds(j * per, per)],
            send_sem=fsend.at[slot],
            recv_sem=frecv.at[lax.rem(slot, nmb)],
            device_id=target(slot),
            device_id_type=MESH,
        )

    def bcopy(k, j):
        return pltpu.make_async_remote_copy(
            src_ref=gout.at[k, pl.ds(j * per, per)],
            dst_ref=gbuf.at[k + offset, pl.ds(j * per, per)],
            send_sem=bsend.at[k],
            recv_sem=brecv.at[k + offset],
            device_id=down,
            device_id_type=MESH,
        )

    def fsent(slot):
        pltpu.make_async_remote_copy(
            src_ref=fout.at[slot], dst_ref=hbuf.at[lax.rem(slot, nmb)], send_sem=fsend.at[slot],
            recv_sem=frecv.at[lax.rem(slot, nmb)], device_id=target(slot), device_id_type=MESH,
        ).wait_send()

    def fgot(k):
        pltpu.make_async_remote_copy(
            src_ref=fout.at[k], dst_ref=hbuf.at[k], send_sem=fsend.at[k], recv_sem=frecv.at[k],
            device_id=target(k), device_id_type=MESH,
        ).wait_recv()

    def bsent(k):
        pltpu.make_async_remote_copy(
            src_ref=gout.at[k], dst_ref=gbuf.at[k + offset], send_sem=bsend.at[k], recv_sem=brecv.at[k + offset],
            device_id=down, device_id_type=MESH,
        ).wait_send()

    def bgot(slot):
        pltpu.make_async_remote_copy(
            src_ref=gout.at[lax.rem(slot, nmb)], dst_ref=gbuf.at[slot], send_sem=bsend.at[lax.rem(slot, nmb)],
            recv_sem=brecv.at[slot], device_id=down, device_id_type=MESH,
        ).wait_recv()

    def dcopy(slot):
        place = lax.rem(slot + nmb, 2 * nmb)
        return pltpu.make_async_remote_copy(
            src_ref=dzb.at[slot], dst_ref=dzb.at[place], send_sem=dsend.at[slot], recv_sem=drecv.at[place],
            device_id=mate, device_id_type=MESH,
        )

    def dgot(slot):
        pltpu.make_async_remote_copy(
            src_ref=dzb.at[slot], dst_ref=dzb.at[slot], send_sem=dsend.at[slot], recv_sem=drecv.at[slot],
            device_id=mate, device_id_type=MESH,
        ).wait_recv()

    def ucopy(h):
        return pltpu.make_async_remote_copy(
            src_ref=uts.at[h], dst_ref=ub.at[1 - h], send_sem=us.at[h], recv_sem=ur.at[1 - h],
            device_id=mate, device_id_type=MESH,
        )

    def setup():
        ia = lax.broadcasted_iota(jnp.int32, (nt, nt), 0)
        ib = lax.broadcasted_iota(jnp.int32, (nt, nt), 1)
        across = jnp.broadcast_to(line_ref[...], (nt, nt))
        down_col = jnp.sum(jnp.where(ia == ib, across, 0), axis=1, keepdims=True)
        along = jnp.broadcast_to(down_col, (nt, nt))
        ahead = (across < along) | ((across == along) & (ib < ia))
        rank = jnp.broadcast_to(jnp.sum(jnp.where(ahead, 1, 0), axis=1, keepdims=True), (nt, nt))
        here = rank == ib
        perm = jnp.sum(jnp.where(here, ia, 0), axis=0, keepdims=True)
        ordered = jnp.sum(jnp.where(here, along, 0), axis=0, keepdims=True)
        previous = jnp.sum(jnp.where(rank == ib - 1, along + 1, 0), axis=0, keepdims=True) - 1
        upto = jnp.sum(jnp.where(along <= ib, 1, 0), axis=0, keepdims=True)
        count = jnp.sum(jnp.where(along == ib, 1, 0), axis=0, keepdims=True)
        last = jnp.maximum(upto - 1, 0)
        board[0:1, 0:nt] = perm
        board[1:2, 0:nt] = jnp.where(ordered == previous, 1, 0)
        board[2:3, 0:nt] = last
        board[3:4, 0:nt] = jnp.where(count > 0, 1, 0)
        for j in range(CHAINS - 1):
            end = run * j + run - 1
            spans = (count > 0) & (upto - count <= end) & (last > end)
            board[4 + j:5 + j, 0:nt] = jnp.where(spans, 1, 0)
        copy = pltpu.make_async_copy(board, table, tsem)
        copy.start()

        def turn(c, carry):
            for i in range(3):
                flip[c, :, i * 128:(i + 1) * 128] = t_ref[c, i * 128:(i + 1) * 128, :].T
            return carry

        lax.fori_loop(0, nb, turn, 0)
        copy.wait()

    def turned(h):
        order = arrange(gx, gy)

        def one(b, carry):
            q = hbuf[h * nmb:(h + 1) * nmb, b].astype(F32) * scl[h * nmb:(h + 1) * nmb]
            u = q.reshape(nmb * MB, 128).astype(BF16)
            moved = lax.dot_general(order, u, (((1,), (1,)), ((), ())), preferred_element_type=F32)
            moved = moved.astype(BF16)
            ub[h, b] = moved[:64]
            uts[h, b] = moved[64:]
            return carry

        lax.fori_loop(0, nb, one, 0)
        ucopy(h).start()

    def forward(k, carry):
        @pl.when(first & (k < nmb))
        def _():
            hbuf[k] = x_ref[lax.rem(k, nmb)]

        @pl.when(first & (k >= nmb))
        def _():
            xcopy(k - nmb).wait_recv()

        @pl.when(sec > 0)
        def _():
            fgot(k)

        total = jnp.zeros((MB, 128), F32)
        for b in range(nb):
            h = hbuf[k, b]
            hf = h.astype(F32)
            total = total + hf * hf
            hw[b] = h
        mean = jnp.sum(total, axis=1, keepdims=True) * (1.0 / width)
        scale = jnp.broadcast_to(lax.rsqrt(mean + EPS), (MB, 128))
        scl[k] = scale
        for c in range(nb):
            left = jnp.concatenate([hw[rows_ref[3 * c + i]] for i in range(3)], axis=1)
            z = jnp.dot(left, t_ref[c], preferred_element_type=F32)
            a = jnp.tanh(z * scale)
            act[k, c] = 1.0 - a * a
            fout[k, c] = (hbuf[k, c].astype(F32) + a).astype(BF16)
            if (c + 1) % per == 0:
                @pl.when(sec < sections - 1)
                def _(j=c // per):
                    fcopy(k, j).start()
        return carry

    def ending(k, carry):
        bgot(k)
        for c in range(nb):
            dzb[k, c] = (gbuf[k, c].astype(F32) * act[k, c]).astype(BF16)
        dcopy(k).start()
        return carry

    def backward(k, carry):
        @pl.when(final)
        def _():
            gbuf[k] = og_ref[k]

        @pl.when(sec < sections - 1)
        def _():
            bgot(k)

        for c in range(nb):
            dz = (gbuf[k, c].astype(F32) * act[k, c]).astype(BF16)
            dzb[k, c] = dz
            back = jnp.dot(dz, flip[c], preferred_element_type=F32)
            for i in range(3):
                prod[3 * c + i] = back[:, i * 128:(i + 1) * 128]
        scale = scl[k]
        for j in range(CHAINS):
            acc = prod[table[0, run * j]]
            pref[run * j] = acc
            for i in range(run * j + 1, run * j + run):
                acc = acc * table[1, i].astype(F32) + prod[table[0, i]]
                pref[i] = acc
        inner = jnp.zeros((MB, 128), F32)
        for b in range(nb):
            q = hbuf[k, b].astype(F32) * scale
            v = pref[table[2, b]] * table[3, b].astype(F32)
            for j in range(CHAINS - 1):
                v = v + pref[run * j + run - 1] * table[4 + j, b].astype(F32)
            inner = inner + v * q
            prod[b] = v
        inner = jnp.sum(inner, axis=1, keepdims=True) * (1.0 / width)
        inner = jnp.broadcast_to(inner, (MB, 128))
        for b in range(nb):
            q = hbuf[k, b].astype(F32) * scale
            g = gbuf[k, b].astype(F32) + scale * (prod[b] - q * inner)
            gout[k, b] = g.astype(BF16)
            if (b + 1) % per == 0:
                bcopy(k, b // per).start()
        dcopy(k).start()
        return carry

    early = sec >= sections // 2
    late = jnp.logical_not(early | first)
    warm = jnp.minimum(1 + AHEAD * (sections - 1 - sec), nmb)
    rounds = jnp.where(first, jnp.where(odd, 2 * nmb, 0), warm)
    paired = jnp.where(first, 0, nmb - warm)

    @pl.when(early)
    def _():
        setup()

    def opening(i, carry):
        j = i - LAG
        mixed = jnp.where(lax.rem(j, 2) == 0, nmb + j // 2, LAG + j // 2)
        mixed = jnp.where(i < LAG, i, jnp.where(i >= 2 * nmb - LAG, i, mixed))
        return forward(jnp.where(first, mixed, i), carry)

    lax.fori_loop(0, rounds, opening, 0)

    @pl.when(late)
    def _():
        setup()
        turned(0)

    @pl.when(worker)
    def _():
        pl.semaphore_wait(ready, 1)
        turned(0)
        turned(1)

    def both(k, carry):
        backward(k, carry)
        forward(k + warm, carry)
        return carry

    lax.fori_loop(0, paired, both, 0)

    @pl.when(sec > 0)
    def _():
        lax.fori_loop(nmb - warm, nmb, backward, 0)

    @pl.when(worker)
    def _():
        def alternate(i, carry):
            return ending(i // 2 + nmb * lax.rem(i, 2), carry)

        lax.fori_loop(0, 2 * nmb, alternate, 0)

    @pl.when(early)
    def _():
        turned(0)

    @pl.when(idle)
    def _():
        ucopy(1).wait_recv()

    @pl.when(jnp.logical_not(worker))
    def _():
        ucopy(0).wait_recv()

    def arrived(k, carry):
        dgot(k)
        return carry

    lax.fori_loop(jnp.where(first, jnp.where(odd, 2 * nmb, 0), nmb), 2 * nmb, arrived, 0)

    low, high = pl.ds(0, half), pl.ds(half, half)

    def copy1(g, kind):
        src, dst, peer = (
            (so.at[g, low], ro.at[g, 0], right),
            (so.at[g, high], ro.at[g, 1], left),
            (sr.at[g, high], got1.at[g, 0, high], right),
            (sl.at[g, low], got1.at[g, 1, low], left),
            (sr.at[g, low], got1.at[g, 0, low], right),
            (sl.at[g, high], got1.at[g, 1, high], left),
        )[kind]
        return pltpu.make_async_remote_copy(
            src_ref=src, dst_ref=dst, send_sem=s1.at[g, kind], recv_sem=r1.at[g, kind],
            device_id=peer, device_id_type=MESH,
        )

    def copy2(g, j):
        return pltpu.make_async_remote_copy(
            src_ref=sy.at[g, lax.rem(me_y + j, gy)], dst_ref=got2.at[g, j - 1],
            send_sem=s2.at[g, j - 1], recv_sem=r2.at[g, j - 1],
            device_id=ys[j - 1], device_id_type=MESH,
        )

    for g in range(GROUPS):
        def column(c, carry, g=g):
            col = g * (tper // 3) + c
            d = dzb[:, col].astype(F32).reshape(2 * nmb * MB, 128).astype(BF16)
            for i in range(3):
                row = rows_ref[3 * col + i]
                wide = jnp.concatenate([ub[0, row], ub[1, row]], axis=1)
                full = jnp.dot(wide, d, preferred_element_type=F32)
                for x in range(gx):
                    own[g, x, 3 * c + i] = full[x * rx:(x + 1) * rx]
            return carry

        lax.fori_loop(0, tper // 3, column, 0)

        def over(t, carry, g=g):
            so[g, t] = own[g, x_over, t].astype(BF16)
            return carry

        def straight(t, carry, g=g):
            sr[g, half + t] = own[g, x_right, half + t].astype(BF16)
            sl[g, t] = own[g, x_left, t].astype(BF16)
            return carry

        lax.fori_loop(0, tper, over, 0, unroll=4)
        copy1(g, 0).start()
        copy1(g, 1).start()
        lax.fori_loop(0, half, straight, 0, unroll=4)
        copy1(g, 2).start()
        copy1(g, 3).start()

    for g in range(GROUPS):
        copy1(g, 0).wait_recv()
        copy1(g, 1).wait_recv()

        def carried(t, carry, g=g):
            sr[g, t] = (own[g, x_right, t] + ro[g, 0, t].astype(F32)).astype(BF16)
            sl[g, half + t] = (own[g, x_left, half + t] + ro[g, 1, t].astype(F32)).astype(BF16)
            return carry

        lax.fori_loop(0, half, carried, 0, unroll=4)
        copy1(g, 4).start()
        copy1(g, 5).start()

    a = lax.broadcasted_iota(jnp.int32, (8 * rx, 8 * rx), 0)
    b = lax.broadcasted_iota(jnp.int32, (8 * rx, 8 * rx), 1)
    src = lax.rem(a, 8) * rx + (a // (8 * ni)) * ni + lax.rem(a // 8, ni)
    mix = jnp.where(b == src, 1.0, 0.0).astype(BF16)

    for g in range(GROUPS):
        for kind in range(2, 6):
            copy1(g, kind).wait_recv()

        def block(q, carry, g=g):
            pieces = []
            for t in range(8):
                s = own[g, me_x, q * 8 + t]
                for j in range(2):
                    s = s + got1[g, j, q * 8 + t].astype(F32)
                pieces.append(s)
            s = jnp.concatenate(pieces, axis=0).astype(BF16)
            moved = jnp.dot(mix, s, preferred_element_type=F32).astype(BF16)
            for y in range(gy):
                sy[g, y, q] = moved[y * 8 * ni:(y + 1) * 8 * ni]
            return carry

        lax.fori_loop(0, sub, block, 0)
        for j in range(1, gy):
            copy2(g, j).start()

    for g in range(GROUPS):
        for j in range(1, gy):
            copy2(g, j).wait_recv()
        for q in range(sub):
            s = sy[g, me_y, q].astype(F32)
            for j in range(gy - 1):
                s = s + got2[g, j, q].astype(F32)
            for i in range(ni):
                out_ref[i, (g * sub + q) * 8:(g * sub + q + 1) * 8, :] = s[i * 8:(i + 1) * 8]

    for g in range(GROUPS):
        for kind in range(6):
            copy1(g, kind).wait_send()
        for j in range(1, gy):
            copy2(g, j).wait_send()

    @pl.when(jnp.logical_not(idle))
    def _():
        ucopy(0).wait_send()

    @pl.when(worker)
    def _():
        ucopy(1).wait_send()

    def fdrain(k, carry):
        fsent(k)
        return carry

    def bdrain(k, carry):
        bsent(k)
        return carry

    def ddrain(k, carry):
        dcopy(k).wait_send()
        return carry

    def xdrain(k, carry):
        xcopy(k).wait_send()
        return carry

    sent = jnp.where(first, jnp.where(odd, 2 * nmb, 0), nmb)
    lax.fori_loop(0, jnp.where(final, 0, sent), fdrain, 0)
    lax.fori_loop(0, jnp.where(first, 0, nmb), bdrain, 0)
    lax.fori_loop(0, sent, ddrain, 0)
    lax.fori_loop(0, jnp.where(feeder, nmb, 0), xdrain, 0)


def local(gx, gy, inputs, tiles, tile_rows, out_grad):
    sections = lax.axis_size("section")
    rows = tile_rows[0]
    total, width = inputs.shape
    nb = width // 128
    nt = tiles.shape[1]
    nmb = total // MB
    feed = inputs.reshape(nmb, MB, nb, 128).transpose(0, 2, 1, 3)
    seeds = out_grad.reshape(nmb, MB, nb, 128).transpose(0, 2, 1, 3)
    tall = tiles.reshape(nb, 3 * 128, 128)
    smem = pl.BlockSpec(memory_space=pltpu.SMEM)
    vmem = pl.BlockSpec(memory_space=pltpu.VMEM)
    dma = pltpu.SemaphoreType.DMA
    piece = (nmb, nb, MB, 128)
    ni = 128 // (2 * gx * gy)
    rx = gy * ni
    tper = nt // GROUPS
    strip = (2, nb, 64, nmb * MB)
    twice = (2 * nmb, nb, MB, 128)
    return pl.pallas_call(
        functools.partial(relay_kernel, sections, nmb, nb, gx, gy),
        out_shape=jax.ShapeDtypeStruct((ni, nt, 128), F32),
        in_specs=[smem] + [vmem] * 4,
        out_specs=vmem,
        scratch_shapes=[
            pltpu.VMEM(twice, BF16),
            pltpu.VMEM(strip, BF16), pltpu.VMEM(strip, BF16),
            pltpu.VMEM((GROUPS, gx, tper, rx, 128), F32),
            pltpu.VMEM((GROUPS, tper, rx, 128), BF16),
            pltpu.VMEM((GROUPS, tper, rx, 128), BF16),
            pltpu.VMEM((GROUPS, tper, rx, 128), BF16),
            pltpu.VMEM((GROUPS, 2, tper // 2, rx, 128), BF16),
            pltpu.VMEM((GROUPS, 2, tper, rx, 128), BF16),
            pltpu.VMEM((GROUPS, gy, tper // 8, 8 * ni, 128), BF16),
            pltpu.VMEM((GROUPS, gy - 1, tper // 8, 8 * ni, 128), BF16),
            pltpu.VMEM(twice, BF16), pltpu.VMEM(twice, BF16), pltpu.VMEM(twice, BF16), pltpu.VMEM(piece, BF16),
            pltpu.VMEM((nb, MB, 128), BF16),
            pltpu.VMEM(twice, F32),
            pltpu.VMEM((2 * nmb, MB, 128), F32),
            pltpu.VMEM((nt, MB, 128), F32),
            pltpu.VMEM((nt, MB, 128), F32),
            pltpu.VMEM((nb, 128, 3 * 128), BF16),
            pltpu.VMEM((8, 128), jnp.int32),
            pltpu.SMEM((8, 128), jnp.int32),
            dma(()),
            dma((2 * nmb,)), dma((nmb,)), dma((nmb,)), dma((2 * nmb,)), dma((2 * nmb,)), dma((2 * nmb,)),
            dma((2,)), dma((2,)),
            dma((GROUPS, 6)), dma((GROUPS, 6)),
            dma((GROUPS, gy - 1)), dma((GROUPS, gy - 1)),
            dma((nmb,)), dma((nmb,)), pltpu.SemaphoreType.REGULAR, pltpu.SemaphoreType.REGULAR,
        ],
        compiler_params=pltpu.CompilerParams(collective_id=0, has_side_effects=True),
        name="relay",
    )(rows, tile_rows, feed, tall, seeds).reshape(ni, 1, nt, 128)


def solution(mesh, gx=GRID_X, gy=GRID_Y):
    return jax.shard_map(
        functools.partial(local, gx, gy),
        mesh=mesh,
        in_specs=(P("dp", None), P("section", None, None, None), P("section", None), P("dp", None)),
        out_specs=P("dp", "section", None, None),
        check_vma=False,
    )
```

```python
import functools

import jax
import jax.numpy as jnp
from jax import lax
from jax.experimental import pallas as pl
from jax.experimental.pallas import tpu as pltpu
from jax.sharding import PartitionSpec as P

EPS = 1e-06
MB = 8
CHUNKS = 2
CHAINS = 2
AHEAD = 6
LAG = 4
GRID_X = 4
GRID_Y = 8
GROUPS = 3
MESH = pl.DeviceIdType.MESH
F32 = jnp.float32
BF16 = jnp.bfloat16


def arrange(gx, gy):
    ni = 128 // (2 * gx * gy)
    rx = gy * ni
    side = lax.rem(lax.axis_index("dp"), 2)
    p = lax.broadcasted_iota(jnp.int32, (128, 128), 0)
    r = lax.broadcasted_iota(jnp.int32, (128, 128), 1)
    far = p // 64
    core = far + side - 2 * far * side
    px = lax.rem(p // rx, gx)
    py = lax.rem(p // ni, gy)
    want = ((py * gx + px) * 2 + core) * ni + lax.rem(p, ni)
    return jnp.where(r == want, 1.0, 0.0).astype(BF16)


def relay_kernel(sections, nmb, nb, gx, gy, rows_ref, line_ref, x_ref, t_ref, og_ref,
                 out_ref,
                 dzb, ub, uts, own, so, sr, sl, ro, got1, sy, got2,
                 hbuf, gbuf, fout, gout, hw, duo, act, scl, prod, pref, flip, board, table, tsem,
                 fsend, frecv, bsend, brecv, dsend, drecv, us, ur, s1, r1, s2, r2, xsend, xrecv, ready):
    sec = lax.axis_index("section")
    dp = lax.axis_index("dp")
    nt = 3 * nb
    width = nb * 128
    per = nb // CHUNKS
    run = nt // CHAINS
    ni = 128 // (2 * gx * gy)
    rx = gy * ni
    tper = nt // GROUPS
    half = tper // 2
    sub = tper // 8
    me_c = lax.rem(dp, 2)
    me_x = lax.rem(dp // 2, gx)
    me_y = dp // (2 * gx)
    first = sec == 0
    final = sec == sections - 1
    odd = me_c == 1
    worker = first & odd
    idle = first & jnp.logical_not(odd)
    feeder = (sec == 1) & jnp.logical_not(odd)
    swap = dp + 1 - 2 * me_c
    straight = sections - 1 - lax.rem(sections - 1, 2)
    above = jnp.minimum(sec + 1, sections - 1)
    below = jnp.maximum(sec - 1, 0)
    up_dp = jnp.where(sec < straight, swap, dp)
    down_dp = jnp.where(sec == 1, dp + 1 - me_c, jnp.where(sec - 1 < straight, swap, dp))
    offset = jnp.where((sec == 1) & odd, nmb, 0)
    down = {"dp": down_dp, "section": below}
    mate = {"dp": swap}

    def at(y, x):
        return {"dp": (y * gx + x) * 2 + me_c}

    x_right = lax.rem(me_x + 1, gx)
    x_left = lax.rem(me_x + gx - 1, gx)
    x_over = lax.rem(me_x + 2, gx)
    right = at(me_y, x_right)
    left = at(me_y, x_left)
    ys = [at(lax.rem(me_y + j, gy), me_x) for j in range(1, gy)]

    barrier = pltpu.get_barrier_semaphore()

    def greet(peer):
        pl.semaphore_signal(barrier, inc=1, device_id=peer, device_id_type=MESH)

    @pl.when(sec > 0)
    def _():
        greet(down)

    @pl.when((sec > 0) & (sec < sections - 1))
    def _():
        greet({"dp": up_dp, "section": above})

    @pl.when(worker)
    def _():
        greet({"dp": swap, "section": above})
        greet({"dp": dp, "section": above})

    for peer in [left, right] + ys:
        greet(peer)

    @pl.when(jnp.logical_not(idle))
    def _():
        greet(mate)

    count = gy + 1 + jnp.where(first, jnp.where(odd, 2, 1), 2 + jnp.where(final, 0, 1))
    pl.semaphore_wait(barrier, count)

    @pl.when(idle)
    def _():
        pl.semaphore_signal(ready, inc=1, device_id=mate, device_id_type=MESH)

    def xcopy(k):
        return pltpu.make_async_remote_copy(
            src_ref=x_ref.at[k], dst_ref=hbuf.at[nmb + k], send_sem=xsend.at[k], recv_sem=xrecv.at[k],
            device_id={"dp": dp + 1 - me_c, "section": below}, device_id_type=MESH,
        )

    @pl.when(feeder)
    def _():
        def feed(k, carry):
            xcopy(k).start()
            return carry

        lax.fori_loop(0, nmb, feed, 0)

    def target(slot):
        return {"dp": jnp.where(first & (slot >= nmb), dp, up_dp), "section": above}

    def fcopy(slot, j):
        return pltpu.make_async_remote_copy(
            src_ref=fout.at[slot, pl.ds(j * per, per)],
            dst_ref=hbuf.at[lax.rem(slot, nmb), pl.ds(j * per, per)],
            send_sem=fsend.at[slot],
            recv_sem=frecv.at[lax.rem(slot, nmb)],
            device_id=target(slot),
            device_id_type=MESH,
        )

    def bcopy(k, j):
        return pltpu.make_async_remote_copy(
            src_ref=gout.at[k, pl.ds(j * per, per)],
            dst_ref=gbuf.at[k + offset, pl.ds(j * per, per)],
            send_sem=bsend.at[k],
            recv_sem=brecv.at[k + offset],
            device_id=down,
            device_id_type=MESH,
        )

    def fsent(slot):
        pltpu.make_async_remote_copy(
            src_ref=fout.at[slot], dst_ref=hbuf.at[lax.rem(slot, nmb)], send_sem=fsend.at[slot],
            recv_sem=frecv.at[lax.rem(slot, nmb)], device_id=target(slot), device_id_type=MESH,
        ).wait_send()

    def fgot(k):
        pltpu.make_async_remote_copy(
            src_ref=fout.at[k], dst_ref=hbuf.at[k], send_sem=fsend.at[k], recv_sem=frecv.at[k],
            device_id=target(k), device_id_type=MESH,
        ).wait_recv()

    def bsent(k):
        pltpu.make_async_remote_copy(
            src_ref=gout.at[k], dst_ref=gbuf.at[k + offset], send_sem=bsend.at[k], recv_sem=brecv.at[k + offset],
            device_id=down, device_id_type=MESH,
        ).wait_send()

    def bgot(slot):
        pltpu.make_async_remote_copy(
            src_ref=gout.at[lax.rem(slot, nmb)], dst_ref=gbuf.at[slot], send_sem=bsend.at[lax.rem(slot, nmb)],
            recv_sem=brecv.at[slot], device_id=down, device_id_type=MESH,
        ).wait_recv()

    def dcopy(slot):
        place = lax.rem(slot + nmb, 2 * nmb)
        return pltpu.make_async_remote_copy(
            src_ref=dzb.at[slot], dst_ref=dzb.at[place], send_sem=dsend.at[slot], recv_sem=drecv.at[place],
            device_id=mate, device_id_type=MESH,
        )

    def dgot(slot):
        pltpu.make_async_remote_copy(
            src_ref=dzb.at[slot], dst_ref=dzb.at[slot], send_sem=dsend.at[slot], recv_sem=drecv.at[slot],
            device_id=mate, device_id_type=MESH,
        ).wait_recv()

    def ucopy(h):
        return pltpu.make_async_remote_copy(
            src_ref=uts.at[h], dst_ref=ub.at[1 - h], send_sem=us.at[h], recv_sem=ur.at[1 - h],
            device_id=mate, device_id_type=MESH,
        )

    def setup():
        ia = lax.broadcasted_iota(jnp.int32, (nt, nt), 0)
        ib = lax.broadcasted_iota(jnp.int32, (nt, nt), 1)
        across = jnp.broadcast_to(line_ref[...], (nt, nt))
        down_col = jnp.sum(jnp.where(ia == ib, across, 0), axis=1, keepdims=True)
        along = jnp.broadcast_to(down_col, (nt, nt))
        ahead = (across < along) | ((across == along) & (ib < ia))
        rank = jnp.broadcast_to(jnp.sum(jnp.where(ahead, 1, 0), axis=1, keepdims=True), (nt, nt))
        here = rank == ib
        perm = jnp.sum(jnp.where(here, ia, 0), axis=0, keepdims=True)
        ordered = jnp.sum(jnp.where(here, along, 0), axis=0, keepdims=True)
        previous = jnp.sum(jnp.where(rank == ib - 1, along + 1, 0), axis=0, keepdims=True) - 1
        upto = jnp.sum(jnp.where(along <= ib, 1, 0), axis=0, keepdims=True)
        count = jnp.sum(jnp.where(along == ib, 1, 0), axis=0, keepdims=True)
        last = jnp.maximum(upto - 1, 0)
        board[0:1, 0:nt] = perm
        board[1:2, 0:nt] = jnp.where(ordered == previous, 1, 0)
        board[2:3, 0:nt] = last
        board[3:4, 0:nt] = jnp.where(count > 0, 1, 0)
        for j in range(CHAINS - 1):
            end = run * j + run - 1
            spans = (count > 0) & (upto - count <= end) & (last > end)
            board[4 + j:5 + j, 0:nt] = jnp.where(spans, 1, 0)
        copy = pltpu.make_async_copy(board, table, tsem)
        copy.start()

        def turn(c, carry):
            for i in range(3):
                for e in range(2):
                    flip[c, e * 128:(e + 1) * 128, i * 128:(i + 1) * 128] = t_ref[2 * c + e, i * 128:(i + 1) * 128, :].T
            return carry

        lax.fori_loop(0, nb // 2, turn, 0)
        copy.wait()

    def turned(h):
        order = arrange(gx, gy)

        def one(b, carry):
            q = hbuf[h * nmb:(h + 1) * nmb, b].astype(F32) * scl[h * nmb:(h + 1) * nmb]
            u = q.reshape(nmb * MB, 128).astype(BF16)
            moved = lax.dot_general(order, u, (((1,), (1,)), ((), ())), preferred_element_type=F32)
            moved = moved.astype(BF16)
            ub[h, b] = moved[:64]
            uts[h, b] = moved[64:]
            return carry

        lax.fori_loop(0, nb, one, 0)
        ucopy(h).start()

    def forward(k, carry):
        @pl.when(first & (k < nmb))
        def _():
            hbuf[k] = x_ref[lax.rem(k, nmb)]

        @pl.when(first & (k >= nmb))
        def _():
            xcopy(k - nmb).wait_recv()

        @pl.when(sec > 0)
        def _():
            fgot(k)

        total = jnp.zeros((MB, 128), F32)
        for b in range(nb):
            h = hbuf[k, b]
            hf = h.astype(F32)
            total = total + hf * hf
            hw[b] = hf
        mean = jnp.sum(total, axis=1, keepdims=True) * (1.0 / width)
        scale = jnp.broadcast_to(lax.rsqrt(mean + EPS), (MB, 128))
        scl[k] = scale
        for c in range(nb):
            if c % 2 == 0:
                left = jnp.concatenate(
                    [jnp.concatenate([hw[rows_ref[3 * c + i]], hw[rows_ref[3 * c + 3 + i]]], axis=0) for i in range(3)],
                    axis=1,
                ).astype(BF16)
                wide = jnp.dot(left, duo[c // 2], preferred_element_type=F32)
            z = wide[(c % 2) * MB:(c % 2 + 1) * MB, (c % 2) * 128:(c % 2 + 1) * 128]
            a = jnp.tanh(z * scale)
            act[k, c] = 1.0 - a * a
            fout[k, c] = (hbuf[k, c].astype(F32) + a).astype(BF16)
            if (c + 1) % per == 0:
                @pl.when(sec < sections - 1)
                def _(j=c // per):
                    fcopy(k, j).start()
        return carry

    def ending(k, carry):
        bgot(k)
        for c in range(nb):
            dzb[k, c] = (gbuf[k, c].astype(F32) * act[k, c]).astype(BF16)
        dcopy(k).start()
        return carry

    def backward(k, carry):
        @pl.when(final)
        def _():
            gbuf[k] = og_ref[k]

        @pl.when(sec < sections - 1)
        def _():
            bgot(k)

        blank = jnp.zeros((MB, 128), F32)
        for c in range(0, nb, 2):
            both_dz = []
            for e in range(2):
                dz = (gbuf[k, c + e].astype(F32) * act[k, c + e]).astype(BF16)
                dzb[k, c + e] = dz
                both_dz.append(dz.astype(F32))
            upper = jnp.concatenate([both_dz[0], blank], axis=0)
            lower = jnp.concatenate([blank, both_dz[1]], axis=0)
            wide = jnp.concatenate([upper, lower], axis=1).astype(BF16)
            back = jnp.dot(wide, flip[c // 2], preferred_element_type=F32)
            for i in range(3):
                prod[3 * c + i] = back[:MB, i * 128:(i + 1) * 128]
                prod[3 * c + 3 + i] = back[MB:, i * 128:(i + 1) * 128]
        scale = scl[k]
        for j in range(CHAINS):
            acc = prod[table[0, run * j]]
            pref[run * j] = acc
            for i in range(run * j + 1, run * j + run):
                acc = acc * table[1, i].astype(F32) + prod[table[0, i]]
                pref[i] = acc
        inner = jnp.zeros((MB, 128), F32)
        for b in range(nb):
            q = hbuf[k, b].astype(F32) * scale
            v = pref[table[2, b]] * table[3, b].astype(F32)
            for j in range(CHAINS - 1):
                v = v + pref[run * j + run - 1] * table[4 + j, b].astype(F32)
            inner = inner + v * q
            prod[b] = v
        inner = jnp.sum(inner, axis=1, keepdims=True) * (1.0 / width)
        inner = jnp.broadcast_to(inner, (MB, 128))
        for b in range(nb):
            q = hbuf[k, b].astype(F32) * scale
            g = gbuf[k, b].astype(F32) + scale * (prod[b] - q * inner)
            gout[k, b] = g.astype(BF16)
            if (b + 1) % per == 0:
                bcopy(k, b // per).start()
        dcopy(k).start()
        return carry

    def pair(c, carry):
        duo[c, :, :128] = t_ref[2 * c]
        duo[c, :, 128:] = t_ref[2 * c + 1]
        return carry

    lax.fori_loop(0, nb // 2, pair, 0)
    early = sec >= sections // 2
    late = jnp.logical_not(early | first)
    warm = jnp.minimum(1 + AHEAD * (sections - 1 - sec), nmb)
    rounds = jnp.where(first, jnp.where(odd, 2 * nmb, 0), warm)
    paired = jnp.where(first, 0, nmb - warm)

    @pl.when(early)
    def _():
        setup()

    def opening(i, carry):
        j = i - LAG
        mixed = jnp.where(lax.rem(j, 2) == 0, nmb + j // 2, LAG + j // 2)
        mixed = jnp.where(i < LAG, i, jnp.where(i >= 2 * nmb - LAG, i, mixed))
        return forward(jnp.where(first, mixed, i), carry)

    lax.fori_loop(0, rounds, opening, 0)

    @pl.when(late)
    def _():
        setup()
        turned(0)

    @pl.when(worker)
    def _():
        pl.semaphore_wait(ready, 1)
        turned(0)
        turned(1)

    def both(k, carry):
        backward(k, carry)
        forward(k + warm, carry)
        return carry

    lax.fori_loop(0, paired, both, 0)

    @pl.when(sec > 0)
    def _():
        lax.fori_loop(nmb - warm, nmb, backward, 0)

    @pl.when(worker)
    def _():
        def alternate(i, carry):
            return ending(i // 2 + nmb * lax.rem(i, 2), carry)

        lax.fori_loop(0, 2 * nmb, alternate, 0)

    @pl.when(early)
    def _():
        turned(0)

    @pl.when(idle)
    def _():
        ucopy(1).wait_recv()

    @pl.when(jnp.logical_not(worker))
    def _():
        ucopy(0).wait_recv()

    def arrived(k, carry):
        dgot(k)
        return carry

    lax.fori_loop(jnp.where(first, jnp.where(odd, 2 * nmb, 0), nmb), 2 * nmb, arrived, 0)

    low, high = pl.ds(0, half), pl.ds(half, half)

    def copy1(g, kind):
        src, dst, peer = (
            (so.at[g, low], ro.at[g, 0], right),
            (so.at[g, high], ro.at[g, 1], left),
            (sr.at[g, high], got1.at[g, 0, high], right),
            (sl.at[g, low], got1.at[g, 1, low], left),
            (sr.at[g, low], got1.at[g, 0, low], right),
            (sl.at[g, high], got1.at[g, 1, high], left),
        )[kind]
        return pltpu.make_async_remote_copy(
            src_ref=src, dst_ref=dst, send_sem=s1.at[g, kind], recv_sem=r1.at[g, kind],
            device_id=peer, device_id_type=MESH,
        )

    def copy2(g, j):
        return pltpu.make_async_remote_copy(
            src_ref=sy.at[g, lax.rem(me_y + j, gy)], dst_ref=got2.at[g, j - 1],
            send_sem=s2.at[g, j - 1], recv_sem=r2.at[g, j - 1],
            device_id=ys[j - 1], device_id_type=MESH,
        )

    for g in range(GROUPS):
        def column(c, carry, g=g):
            col = g * (tper // 3) + c
            d = dzb[:, col].astype(F32).reshape(2 * nmb * MB, 128).astype(BF16)
            for i in range(3):
                row = rows_ref[3 * col + i]
                wide = jnp.concatenate([ub[0, row], ub[1, row]], axis=1)
                full = jnp.dot(wide, d, preferred_element_type=F32)
                for x in range(gx):
                    own[g, x, 3 * c + i] = full[x * rx:(x + 1) * rx]
            return carry

        lax.fori_loop(0, tper // 3, column, 0)

        def over(t, carry, g=g):
            so[g, t] = own[g, x_over, t].astype(BF16)
            return carry

        def straight(t, carry, g=g):
            sr[g, half + t] = own[g, x_right, half + t].astype(BF16)
            sl[g, t] = own[g, x_left, t].astype(BF16)
            return carry

        lax.fori_loop(0, tper, over, 0, unroll=4)
        copy1(g, 0).start()
        copy1(g, 1).start()
        lax.fori_loop(0, half, straight, 0, unroll=4)
        copy1(g, 2).start()
        copy1(g, 3).start()

    for g in range(GROUPS):
        copy1(g, 0).wait_recv()
        copy1(g, 1).wait_recv()

        def carried(t, carry, g=g):
            sr[g, t] = (own[g, x_right, t] + ro[g, 0, t].astype(F32)).astype(BF16)
            sl[g, half + t] = (own[g, x_left, half + t] + ro[g, 1, t].astype(F32)).astype(BF16)
            return carry

        lax.fori_loop(0, half, carried, 0, unroll=4)
        copy1(g, 4).start()
        copy1(g, 5).start()

    a = lax.broadcasted_iota(jnp.int32, (8 * rx, 8 * rx), 0)
    b = lax.broadcasted_iota(jnp.int32, (8 * rx, 8 * rx), 1)
    src = lax.rem(a, 8) * rx + (a // (8 * ni)) * ni + lax.rem(a // 8, ni)
    mix = jnp.where(b == src, 1.0, 0.0).astype(BF16)

    for g in range(GROUPS):
        for kind in range(2, 6):
            copy1(g, kind).wait_recv()

        def block(q, carry, g=g):
            pieces = []
            for t in range(8):
                s = own[g, me_x, q * 8 + t]
                for j in range(2):
                    s = s + got1[g, j, q * 8 + t].astype(F32)
                pieces.append(s)
            s = jnp.concatenate(pieces, axis=0).astype(BF16)
            moved = jnp.dot(mix, s, preferred_element_type=F32).astype(BF16)
            for y in range(gy):
                sy[g, y, q] = moved[y * 8 * ni:(y + 1) * 8 * ni]
            return carry

        lax.fori_loop(0, sub, block, 0)
        for j in range(1, gy):
            copy2(g, j).start()

    for g in range(GROUPS):
        for j in range(1, gy):
            copy2(g, j).wait_recv()
        for q in range(sub):
            s = sy[g, me_y, q].astype(F32)
            for j in range(gy - 1):
                s = s + got2[g, j, q].astype(F32)
            for i in range(ni):
                out_ref[i, (g * sub + q) * 8:(g * sub + q + 1) * 8, :] = s[i * 8:(i + 1) * 8]

    for g in range(GROUPS):
        for kind in range(6):
            copy1(g, kind).wait_send()
        for j in range(1, gy):
            copy2(g, j).wait_send()

    @pl.when(jnp.logical_not(idle))
    def _():
        ucopy(0).wait_send()

    @pl.when(worker)
    def _():
        ucopy(1).wait_send()

    def fdrain(k, carry):
        fsent(k)
        return carry

    def bdrain(k, carry):
        bsent(k)
        return carry

    def ddrain(k, carry):
        dcopy(k).wait_send()
        return carry

    def xdrain(k, carry):
        xcopy(k).wait_send()
        return carry

    sent = jnp.where(first, jnp.where(odd, 2 * nmb, 0), nmb)
    lax.fori_loop(0, jnp.where(final, 0, sent), fdrain, 0)
    lax.fori_loop(0, jnp.where(first, 0, nmb), bdrain, 0)
    lax.fori_loop(0, sent, ddrain, 0)
    lax.fori_loop(0, jnp.where(feeder, nmb, 0), xdrain, 0)


def local(gx, gy, inputs, tiles, tile_rows, out_grad):
    sections = lax.axis_size("section")
    rows = tile_rows[0]
    total, width = inputs.shape
    nb = width // 128
    nt = tiles.shape[1]
    nmb = total // MB
    feed = inputs.reshape(nmb, MB, nb, 128).transpose(0, 2, 1, 3)
    seeds = out_grad.reshape(nmb, MB, nb, 128).transpose(0, 2, 1, 3)
    tall = tiles.reshape(nb, 3 * 128, 128)
    smem = pl.BlockSpec(memory_space=pltpu.SMEM)
    vmem = pl.BlockSpec(memory_space=pltpu.VMEM)
    dma = pltpu.SemaphoreType.DMA
    piece = (nmb, nb, MB, 128)
    ni = 128 // (2 * gx * gy)
    rx = gy * ni
    tper = nt // GROUPS
    strip = (2, nb, 64, nmb * MB)
    twice = (2 * nmb, nb, MB, 128)
    return pl.pallas_call(
        functools.partial(relay_kernel, sections, nmb, nb, gx, gy),
        out_shape=jax.ShapeDtypeStruct((ni, nt, 128), F32),
        in_specs=[smem] + [vmem] * 4,
        out_specs=vmem,
        scratch_shapes=[
            pltpu.VMEM(twice, BF16),
            pltpu.VMEM(strip, BF16), pltpu.VMEM(strip, BF16),
            pltpu.VMEM((GROUPS, gx, tper, rx, 128), F32),
            pltpu.VMEM((GROUPS, tper, rx, 128), BF16),
            pltpu.VMEM((GROUPS, tper, rx, 128), BF16),
            pltpu.VMEM((GROUPS, tper, rx, 128), BF16),
            pltpu.VMEM((GROUPS, 2, tper // 2, rx, 128), BF16),
            pltpu.VMEM((GROUPS, 2, tper, rx, 128), BF16),
            pltpu.VMEM((GROUPS, gy, tper // 8, 8 * ni, 128), BF16),
            pltpu.VMEM((GROUPS, gy - 1, tper // 8, 8 * ni, 128), BF16),
            pltpu.VMEM(twice, BF16), pltpu.VMEM(twice, BF16), pltpu.VMEM(twice, BF16), pltpu.VMEM(piece, BF16),
            pltpu.VMEM((nb, MB, 128), F32),
            pltpu.VMEM((nb // 2, 3 * 128, 256), BF16),
            pltpu.VMEM(twice, F32),
            pltpu.VMEM((2 * nmb, MB, 128), F32),
            pltpu.VMEM((nt, MB, 128), F32),
            pltpu.VMEM((nt, MB, 128), F32),
            pltpu.VMEM((nb // 2, 256, 3 * 128), BF16),
            pltpu.VMEM((8, 128), jnp.int32),
            pltpu.SMEM((8, 128), jnp.int32),
            dma(()),
            dma((2 * nmb,)), dma((nmb,)), dma((nmb,)), dma((2 * nmb,)), dma((2 * nmb,)), dma((2 * nmb,)),
            dma((2,)), dma((2,)),
            dma((GROUPS, 6)), dma((GROUPS, 6)),
            dma((GROUPS, gy - 1)), dma((GROUPS, gy - 1)),
            dma((nmb,)), dma((nmb,)), pltpu.SemaphoreType.REGULAR,
        ],
        compiler_params=pltpu.CompilerParams(collective_id=0, has_side_effects=True),
        name="relay",
    )(rows, tile_rows, feed, tall, seeds).reshape(ni, 1, nt, 128)


def solution(mesh, gx=GRID_X, gy=GRID_Y):
    return jax.shard_map(
        functools.partial(local, gx, gy),
        mesh=mesh,
        in_specs=(P("dp", None), P("section", None, None, None), P("section", None), P("dp", None)),
        out_specs=P("dp", "section", None, None),
        check_vma=False,
    )
```

```python
import functools

import jax
import jax.numpy as jnp
from jax import lax
from jax.experimental import pallas as pl
from jax.experimental.pallas import tpu as pltpu
from jax.sharding import PartitionSpec as P

EPS = 1e-06
MB = 8
CHUNKS = 2
CHAINS = 2
AHEAD = 6
LAG = 4
GRID_X = 4
GRID_Y = 8
GROUPS = 9
MESH = pl.DeviceIdType.MESH
F32 = jnp.float32
BF16 = jnp.bfloat16


def arrange(gx, gy):
    ni = 128 // (2 * gx * gy)
    rx = gy * ni
    side = lax.rem(lax.axis_index("dp"), 2)
    p = lax.broadcasted_iota(jnp.int32, (128, 128), 0)
    r = lax.broadcasted_iota(jnp.int32, (128, 128), 1)
    far = p // 64
    core = far + side - 2 * far * side
    px = lax.rem(p // rx, gx)
    py = lax.rem(p // ni, gy)
    want = ((py * gx + px) * 2 + core) * ni + lax.rem(p, ni)
    return jnp.where(r == want, 1.0, 0.0).astype(BF16)


def relay_kernel(sections, nmb, nb, gx, gy, rows_ref, line_ref, x_ref, t_ref, og_ref,
                 out_ref,
                 dzb, ub, uts, own, so, sr, sl, ro, got1, sy, got2,
                 hbuf, gbuf, fout, gout, hw, duo, act, scl, prod, pref, flip, board, table, tsem,
                 fsend, frecv, bsend, brecv, dsend, drecv, us, ur, s1, r1, s2, r2, xsend, xrecv, ready):
    sec = lax.axis_index("section")
    dp = lax.axis_index("dp")
    nt = 3 * nb
    width = nb * 128
    per = nb // CHUNKS
    run = nt // CHAINS
    ni = 128 // (2 * gx * gy)
    rx = gy * ni
    tper = nt // GROUPS
    half = tper // 2
    sub = tper // 8
    me_c = lax.rem(dp, 2)
    me_x = lax.rem(dp // 2, gx)
    me_y = dp // (2 * gx)
    first = sec == 0
    final = sec == sections - 1
    odd = me_c == 1
    worker = first & odd
    idle = first & jnp.logical_not(odd)
    feeder = (sec == 1) & jnp.logical_not(odd)
    swap = dp + 1 - 2 * me_c
    straight = sections - 1 - lax.rem(sections - 1, 2)
    above = jnp.minimum(sec + 1, sections - 1)
    below = jnp.maximum(sec - 1, 0)
    up_dp = jnp.where(sec < straight, swap, dp)
    down_dp = jnp.where(sec == 1, dp + 1 - me_c, jnp.where(sec - 1 < straight, swap, dp))
    offset = jnp.where((sec == 1) & odd, nmb, 0)
    down = {"dp": down_dp, "section": below}
    mate = {"dp": swap}

    def at(y, x):
        return {"dp": (y * gx + x) * 2 + me_c}

    x_right = lax.rem(me_x + 1, gx)
    x_left = lax.rem(me_x + gx - 1, gx)
    x_over = lax.rem(me_x + 2, gx)
    right = at(me_y, x_right)
    left = at(me_y, x_left)
    ys = [at(lax.rem(me_y + j, gy), me_x) for j in range(1, gy)]

    barrier = pltpu.get_barrier_semaphore()

    def greet(peer):
        pl.semaphore_signal(barrier, inc=1, device_id=peer, device_id_type=MESH)

    @pl.when(sec > 0)
    def _():
        greet(down)

    @pl.when((sec > 0) & (sec < sections - 1))
    def _():
        greet({"dp": up_dp, "section": above})

    @pl.when(worker)
    def _():
        greet({"dp": swap, "section": above})
        greet({"dp": dp, "section": above})

    for peer in [left, right] + ys:
        greet(peer)

    @pl.when(jnp.logical_not(idle))
    def _():
        greet(mate)

    count = gy + 1 + jnp.where(first, jnp.where(odd, 2, 1), 2 + jnp.where(final, 0, 1))
    pl.semaphore_wait(barrier, count)

    @pl.when(idle)
    def _():
        pl.semaphore_signal(ready, inc=1, device_id=mate, device_id_type=MESH)

    def xcopy(k):
        return pltpu.make_async_remote_copy(
            src_ref=x_ref.at[k], dst_ref=hbuf.at[nmb + k], send_sem=xsend.at[k], recv_sem=xrecv.at[k],
            device_id={"dp": dp + 1 - me_c, "section": below}, device_id_type=MESH,
        )

    @pl.when(feeder)
    def _():
        def feed(k, carry):
            xcopy(k).start()
            return carry

        lax.fori_loop(0, nmb, feed, 0)

    def target(slot):
        return {"dp": jnp.where(first & (slot >= nmb), dp, up_dp), "section": above}

    def fcopy(slot, j):
        return pltpu.make_async_remote_copy(
            src_ref=fout.at[slot, pl.ds(j * per, per)],
            dst_ref=hbuf.at[lax.rem(slot, nmb), pl.ds(j * per, per)],
            send_sem=fsend.at[slot],
            recv_sem=frecv.at[lax.rem(slot, nmb)],
            device_id=target(slot),
            device_id_type=MESH,
        )

    def bcopy(k, j):
        return pltpu.make_async_remote_copy(
            src_ref=gout.at[k, pl.ds(j * per, per)],
            dst_ref=gbuf.at[k + offset, pl.ds(j * per, per)],
            send_sem=bsend.at[k],
            recv_sem=brecv.at[k + offset],
            device_id=down,
            device_id_type=MESH,
        )

    def fsent(slot):
        pltpu.make_async_remote_copy(
            src_ref=fout.at[slot], dst_ref=hbuf.at[lax.rem(slot, nmb)], send_sem=fsend.at[slot],
            recv_sem=frecv.at[lax.rem(slot, nmb)], device_id=target(slot), device_id_type=MESH,
        ).wait_send()

    def fgot(k):
        pltpu.make_async_remote_copy(
            src_ref=fout.at[k], dst_ref=hbuf.at[k], send_sem=fsend.at[k], recv_sem=frecv.at[k],
            device_id=target(k), device_id_type=MESH,
        ).wait_recv()

    def bsent(k):
        pltpu.make_async_remote_copy(
            src_ref=gout.at[k], dst_ref=gbuf.at[k + offset], send_sem=bsend.at[k], recv_sem=brecv.at[k + offset],
            device_id=down, device_id_type=MESH,
        ).wait_send()

    def bgot(slot):
        pltpu.make_async_remote_copy(
            src_ref=gout.at[lax.rem(slot, nmb)], dst_ref=gbuf.at[slot], send_sem=bsend.at[lax.rem(slot, nmb)],
            recv_sem=brecv.at[slot], device_id=down, device_id_type=MESH,
        ).wait_recv()

    def dcopy(slot):
        place = lax.rem(slot + nmb, 2 * nmb)
        return pltpu.make_async_remote_copy(
            src_ref=dzb.at[slot], dst_ref=dzb.at[place], send_sem=dsend.at[slot], recv_sem=drecv.at[place],
            device_id=mate, device_id_type=MESH,
        )

    def dgot(slot):
        pltpu.make_async_remote_copy(
            src_ref=dzb.at[slot], dst_ref=dzb.at[slot], send_sem=dsend.at[slot], recv_sem=drecv.at[slot],
            device_id=mate, device_id_type=MESH,
        ).wait_recv()

    def ucopy(h):
        return pltpu.make_async_remote_copy(
            src_ref=uts.at[h], dst_ref=ub.at[1 - h], send_sem=us.at[h], recv_sem=ur.at[1 - h],
            device_id=mate, device_id_type=MESH,
        )

    def setup():
        ia = lax.broadcasted_iota(jnp.int32, (nt, nt), 0)
        ib = lax.broadcasted_iota(jnp.int32, (nt, nt), 1)
        across = jnp.broadcast_to(line_ref[...], (nt, nt))
        down_col = jnp.sum(jnp.where(ia == ib, across, 0), axis=1, keepdims=True)
        along = jnp.broadcast_to(down_col, (nt, nt))
        ahead = (across < along) | ((across == along) & (ib < ia))
        rank = jnp.broadcast_to(jnp.sum(jnp.where(ahead, 1, 0), axis=1, keepdims=True), (nt, nt))
        here = rank == ib
        perm = jnp.sum(jnp.where(here, ia, 0), axis=0, keepdims=True)
        ordered = jnp.sum(jnp.where(here, along, 0), axis=0, keepdims=True)
        previous = jnp.sum(jnp.where(rank == ib - 1, along + 1, 0), axis=0, keepdims=True) - 1
        upto = jnp.sum(jnp.where(along <= ib, 1, 0), axis=0, keepdims=True)
        count = jnp.sum(jnp.where(along == ib, 1, 0), axis=0, keepdims=True)
        last = jnp.maximum(upto - 1, 0)
        board[0:1, 0:nt] = perm
        board[1:2, 0:nt] = jnp.where(ordered == previous, 1, 0)
        board[2:3, 0:nt] = last
        board[3:4, 0:nt] = jnp.where(count > 0, 1, 0)
        for j in range(CHAINS - 1):
            end = run * j + run - 1
            spans = (count > 0) & (upto - count <= end) & (last > end)
            board[4 + j:5 + j, 0:nt] = jnp.where(spans, 1, 0)
        copy = pltpu.make_async_copy(board, table, tsem)
        copy.start()

        def turn(c, carry):
            for i in range(3):
                for e in range(2):
                    flip[c, e * 128:(e + 1) * 128, i * 128:(i + 1) * 128] = t_ref[2 * c + e, i * 128:(i + 1) * 128, :].T
            return carry

        lax.fori_loop(0, nb // 2, turn, 0)
        copy.wait()

    def turned(h):
        order = arrange(gx, gy)

        def one(b, carry):
            q = hbuf[h * nmb:(h + 1) * nmb, b].astype(F32) * scl[h * nmb:(h + 1) * nmb]
            u = q.reshape(nmb * MB, 128).astype(BF16)
            moved = lax.dot_general(order, u, (((1,), (1,)), ((), ())), preferred_element_type=F32)
            moved = moved.astype(BF16)
            ub[h, b] = moved[:64]
            uts[h, b] = moved[64:]
            return carry

        lax.fori_loop(0, nb, one, 0)
        ucopy(h).start()

    def forward(k, carry):
        @pl.when(first & (k < nmb))
        def _():
            hbuf[k] = x_ref[lax.rem(k, nmb)]

        @pl.when(first & (k >= nmb))
        def _():
            xcopy(k - nmb).wait_recv()

        @pl.when(sec > 0)
        def _():
            fgot(k)

        total = jnp.zeros((MB, 128), F32)
        for b in range(nb):
            h = hbuf[k, b]
            hf = h.astype(F32)
            total = total + hf * hf
            hw[b] = hf
        mean = jnp.sum(total, axis=1, keepdims=True) * (1.0 / width)
        scale = jnp.broadcast_to(lax.rsqrt(mean + EPS), (MB, 128))
        scl[k] = scale
        for c in range(nb):
            if c % 2 == 0:
                left = jnp.concatenate(
                    [jnp.concatenate([hw[rows_ref[3 * c + i]], hw[rows_ref[3 * c + 3 + i]]], axis=0) for i in range(3)],
                    axis=1,
                ).astype(BF16)
                wide = jnp.dot(left, duo[c // 2], preferred_element_type=F32)
            z = wide[(c % 2) * MB:(c % 2 + 1) * MB, (c % 2) * 128:(c % 2 + 1) * 128]
            a = jnp.tanh(z * scale)
            act[k, c] = 1.0 - a * a
            fout[k, c] = (hbuf[k, c].astype(F32) + a).astype(BF16)
            if (c + 1) % per == 0:
                @pl.when(sec < sections - 1)
                def _(j=c // per):
                    fcopy(k, j).start()
        return carry

    def ending(k, carry):
        bgot(k)
        for c in range(nb):
            dzb[k, c] = (gbuf[k, c].astype(F32) * act[k, c]).astype(BF16)
        dcopy(k).start()
        return carry

    def backward(k, carry):
        @pl.when(final)
        def _():
            gbuf[k] = og_ref[k]

        @pl.when(sec < sections - 1)
        def _():
            bgot(k)

        blank = jnp.zeros((MB, 128), F32)
        for c in range(0, nb, 2):
            both_dz = []
            for e in range(2):
                dz = (gbuf[k, c + e].astype(F32) * act[k, c + e]).astype(BF16)
                dzb[k, c + e] = dz
                both_dz.append(dz.astype(F32))
            upper = jnp.concatenate([both_dz[0], blank], axis=0)
            lower = jnp.concatenate([blank, both_dz[1]], axis=0)
            wide = jnp.concatenate([upper, lower], axis=1).astype(BF16)
            back = jnp.dot(wide, flip[c // 2], preferred_element_type=F32)
            for i in range(3):
                prod[3 * c + i] = back[:MB, i * 128:(i + 1) * 128]
                prod[3 * c + 3 + i] = back[MB:, i * 128:(i + 1) * 128]
        scale = scl[k]
        for j in range(CHAINS):
            acc = prod[table[0, run * j]]
            pref[run * j] = acc
            for i in range(run * j + 1, run * j + run):
                acc = acc * table[1, i].astype(F32) + prod[table[0, i]]
                pref[i] = acc
        inner = jnp.zeros((MB, 128), F32)
        for b in range(nb):
            q = hbuf[k, b].astype(F32) * scale
            v = pref[table[2, b]] * table[3, b].astype(F32)
            for j in range(CHAINS - 1):
                v = v + pref[run * j + run - 1] * table[4 + j, b].astype(F32)
            inner = inner + v * q
            prod[b] = v
        inner = jnp.sum(inner, axis=1, keepdims=True) * (1.0 / width)
        inner = jnp.broadcast_to(inner, (MB, 128))
        for b in range(nb):
            q = hbuf[k, b].astype(F32) * scale
            g = gbuf[k, b].astype(F32) + scale * (prod[b] - q * inner)
            gout[k, b] = g.astype(BF16)
            if (b + 1) % per == 0:
                bcopy(k, b // per).start()
        dcopy(k).start()
        return carry

    def pair(c, carry):
        duo[c, :, :128] = t_ref[2 * c]
        duo[c, :, 128:] = t_ref[2 * c + 1]
        return carry

    lax.fori_loop(0, nb // 2, pair, 0)
    early = sec >= sections // 2
    late = jnp.logical_not(early | first)
    warm = jnp.minimum(1 + AHEAD * (sections - 1 - sec), nmb)
    rounds = jnp.where(first, jnp.where(odd, 2 * nmb, 0), warm)
    paired = jnp.where(first, 0, nmb - warm)

    @pl.when(early)
    def _():
        setup()

    def opening(i, carry):
        j = i - LAG
        mixed = jnp.where(lax.rem(j, 2) == 0, nmb + j // 2, LAG + j // 2)
        mixed = jnp.where(i < LAG, i, jnp.where(i >= 2 * nmb - LAG, i, mixed))
        return forward(jnp.where(first, mixed, i), carry)

    lax.fori_loop(0, rounds, opening, 0)

    @pl.when(late)
    def _():
        setup()
        turned(0)

    @pl.when(worker)
    def _():
        pl.semaphore_wait(ready, 1)
        turned(0)
        turned(1)

    def both(k, carry):
        backward(k, carry)
        forward(k + warm, carry)
        return carry

    lax.fori_loop(0, paired, both, 0)

    @pl.when(sec > 0)
    def _():
        lax.fori_loop(nmb - warm, nmb, backward, 0)

    @pl.when(worker)
    def _():
        def alternate(i, carry):
            return ending(i // 2 + nmb * lax.rem(i, 2), carry)

        lax.fori_loop(0, 2 * nmb, alternate, 0)

    @pl.when(early)
    def _():
        turned(0)

    @pl.when(idle)
    def _():
        ucopy(1).wait_recv()

    @pl.when(jnp.logical_not(worker))
    def _():
        ucopy(0).wait_recv()

    def arrived(k, carry):
        dgot(k)
        return carry

    lax.fori_loop(jnp.where(first, jnp.where(odd, 2 * nmb, 0), nmb), 2 * nmb, arrived, 0)

    low, high = pl.ds(0, half), pl.ds(half, half)

    def copy1(g, kind):
        src, dst, peer = (
            (so.at[g, low], ro.at[g, 0], right),
            (so.at[g, high], ro.at[g, 1], left),
            (sr.at[g, high], got1.at[g, 0, high], right),
            (sl.at[g, low], got1.at[g, 1, low], left),
            (sr.at[g, low], got1.at[g, 0, low], right),
            (sl.at[g, high], got1.at[g, 1, high], left),
        )[kind]
        return pltpu.make_async_remote_copy(
            src_ref=src, dst_ref=dst, send_sem=s1.at[g, kind], recv_sem=r1.at[g, kind],
            device_id=peer, device_id_type=MESH,
        )

    def copy2(g, j):
        return pltpu.make_async_remote_copy(
            src_ref=sy.at[g, lax.rem(me_y + j, gy)], dst_ref=got2.at[g, j - 1],
            send_sem=s2.at[g, j - 1], recv_sem=r2.at[g, j - 1],
            device_id=ys[j - 1], device_id_type=MESH,
        )

    for g in range(GROUPS):
        def column(c, carry, g=g):
            col = g * tper // 3 + c
            d = dzb[:, col].astype(F32).reshape(2 * nmb * MB, 128).astype(BF16)
            for i in range(3):
                tile = 3 * col + i
                row = rows_ref[tile]
                wide = jnp.concatenate([ub[0, row], ub[1, row]], axis=1)
                full = jnp.dot(wide, d, preferred_element_type=F32)
                for x in range(gx):
                    own[tile // tper, x, lax.rem(tile, tper)] = full[x * rx:(x + 1) * rx]
            return carry

        if g % 3 == 0:
            lax.fori_loop(0, tper, column, 0)

        def over(t, carry, g=g):
            so[g, t] = own[g, x_over, t].astype(BF16)
            return carry

        def straight(t, carry, g=g):
            sr[g, half + t] = own[g, x_right, half + t].astype(BF16)
            sl[g, t] = own[g, x_left, t].astype(BF16)
            return carry

        lax.fori_loop(0, tper, over, 0, unroll=4)
        copy1(g, 0).start()
        copy1(g, 1).start()
        lax.fori_loop(0, half, straight, 0, unroll=4)
        copy1(g, 2).start()
        copy1(g, 3).start()

    for g in range(GROUPS):
        copy1(g, 0).wait_recv()
        copy1(g, 1).wait_recv()

        def carried(t, carry, g=g):
            sr[g, t] = (own[g, x_right, t] + ro[g, 0, t].astype(F32)).astype(BF16)
            sl[g, half + t] = (own[g, x_left, half + t] + ro[g, 1, t].astype(F32)).astype(BF16)
            return carry

        lax.fori_loop(0, half, carried, 0, unroll=4)
        copy1(g, 4).start()
        copy1(g, 5).start()

    a = lax.broadcasted_iota(jnp.int32, (8 * rx, 8 * rx), 0)
    b = lax.broadcasted_iota(jnp.int32, (8 * rx, 8 * rx), 1)
    src = lax.rem(a, 8) * rx + (a // (8 * ni)) * ni + lax.rem(a // 8, ni)
    mix = jnp.where(b == src, 1.0, 0.0).astype(BF16)

    for g in range(GROUPS):
        for kind in range(2, 6):
            copy1(g, kind).wait_recv()

        def block(q, carry, g=g):
            pieces = []
            for t in range(8):
                s = own[g, me_x, q * 8 + t]
                for j in range(2):
                    s = s + got1[g, j, q * 8 + t].astype(F32)
                pieces.append(s)
            s = jnp.concatenate(pieces, axis=0).astype(BF16)
            moved = jnp.dot(mix, s, preferred_element_type=F32).astype(BF16)
            for y in range(gy):
                sy[g, y, q] = moved[y * 8 * ni:(y + 1) * 8 * ni]
            return carry

        lax.fori_loop(0, sub, block, 0)
        for j in range(1, gy):
            copy2(g, j).start()

    for g in range(GROUPS):
        for j in range(1, gy):
            copy2(g, j).wait_recv()
        for q in range(sub):
            s = sy[g, me_y, q].astype(F32)
            for j in range(gy - 1):
                s = s + got2[g, j, q].astype(F32)
            for i in range(ni):
                out_ref[i, (g * sub + q) * 8:(g * sub + q + 1) * 8, :] = s[i * 8:(i + 1) * 8]

    for g in range(GROUPS):
        for kind in range(6):
            copy1(g, kind).wait_send()
        for j in range(1, gy):
            copy2(g, j).wait_send()

    @pl.when(jnp.logical_not(idle))
    def _():
        ucopy(0).wait_send()

    @pl.when(worker)
    def _():
        ucopy(1).wait_send()

    def fdrain(k, carry):
        fsent(k)
        return carry

    def bdrain(k, carry):
        bsent(k)
        return carry

    def ddrain(k, carry):
        dcopy(k).wait_send()
        return carry

    def xdrain(k, carry):
        xcopy(k).wait_send()
        return carry

    sent = jnp.where(first, jnp.where(odd, 2 * nmb, 0), nmb)
    lax.fori_loop(0, jnp.where(final, 0, sent), fdrain, 0)
    lax.fori_loop(0, jnp.where(first, 0, nmb), bdrain, 0)
    lax.fori_loop(0, sent, ddrain, 0)
    lax.fori_loop(0, jnp.where(feeder, nmb, 0), xdrain, 0)


def local(gx, gy, inputs, tiles, tile_rows, out_grad):
    sections = lax.axis_size("section")
    rows = tile_rows[0]
    total, width = inputs.shape
    nb = width // 128
    nt = tiles.shape[1]
    nmb = total // MB
    feed = inputs.reshape(nmb, MB, nb, 128).transpose(0, 2, 1, 3)
    seeds = out_grad.reshape(nmb, MB, nb, 128).transpose(0, 2, 1, 3)
    tall = tiles.reshape(nb, 3 * 128, 128)
    smem = pl.BlockSpec(memory_space=pltpu.SMEM)
    vmem = pl.BlockSpec(memory_space=pltpu.VMEM)
    dma = pltpu.SemaphoreType.DMA
    piece = (nmb, nb, MB, 128)
    ni = 128 // (2 * gx * gy)
    rx = gy * ni
    tper = nt // GROUPS
    strip = (2, nb, 64, nmb * MB)
    twice = (2 * nmb, nb, MB, 128)
    return pl.pallas_call(
        functools.partial(relay_kernel, sections, nmb, nb, gx, gy),
        out_shape=jax.ShapeDtypeStruct((ni, nt, 128), F32),
        in_specs=[smem] + [vmem] * 4,
        out_specs=vmem,
        scratch_shapes=[
            pltpu.VMEM(twice, BF16),
            pltpu.VMEM(strip, BF16), pltpu.VMEM(strip, BF16),
            pltpu.VMEM((GROUPS, gx, tper, rx, 128), F32),
            pltpu.VMEM((GROUPS, tper, rx, 128), BF16),
            pltpu.VMEM((GROUPS, tper, rx, 128), BF16),
            pltpu.VMEM((GROUPS, tper, rx, 128), BF16),
            pltpu.VMEM((GROUPS, 2, tper // 2, rx, 128), BF16),
            pltpu.VMEM((GROUPS, 2, tper, rx, 128), BF16),
            pltpu.VMEM((GROUPS, gy, tper // 8, 8 * ni, 128), BF16),
            pltpu.VMEM((GROUPS, gy - 1, tper // 8, 8 * ni, 128), BF16),
            pltpu.VMEM(twice, BF16), pltpu.VMEM(twice, BF16), pltpu.VMEM(twice, BF16), pltpu.VMEM(piece, BF16),
            pltpu.VMEM((nb, MB, 128), F32),
            pltpu.VMEM((nb // 2, 3 * 128, 256), BF16),
            pltpu.VMEM(twice, F32),
            pltpu.VMEM((2 * nmb, MB, 128), F32),
            pltpu.VMEM((nt, MB, 128), F32),
            pltpu.VMEM((nt, MB, 128), F32),
            pltpu.VMEM((nb // 2, 256, 3 * 128), BF16),
            pltpu.VMEM((8, 128), jnp.int32),
            pltpu.SMEM((8, 128), jnp.int32),
            dma(()),
            dma((2 * nmb,)), dma((nmb,)), dma((nmb,)), dma((2 * nmb,)), dma((2 * nmb,)), dma((2 * nmb,)),
            dma((2,)), dma((2,)),
            dma((GROUPS, 6)), dma((GROUPS, 6)),
            dma((GROUPS, gy - 1)), dma((GROUPS, gy - 1)),
            dma((nmb,)), dma((nmb,)), pltpu.SemaphoreType.REGULAR,
        ],
        compiler_params=pltpu.CompilerParams(collective_id=0, has_side_effects=True),
        name="relay",
    )(rows, tile_rows, feed, tall, seeds).reshape(ni, 1, nt, 128)


def solution(mesh, gx=GRID_X, gy=GRID_Y):
    return jax.shard_map(
        functools.partial(local, gx, gy),
        mesh=mesh,
        in_specs=(P("dp", None), P("section", None, None, None), P("section", None), P("dp", None)),
        out_specs=P("dp", "section", None, None),
        check_vma=False,
    )
```
